32 devices in a mesh: member: 8 (over y, x, core), head: 4 (over z).
Axes of the slice: x: 2, y: 2, z: 4, core: 2. Of those that a mesh axis runs over, the one named last changes fastest.
Arguments:
- hidden: bfloat16 [8, 32, 16, 2880], P('member', 'head'), may hold values from -6 to 6
- joined_weight: bfloat16 [2880, 8, 640], P(None, 'head'), may hold values from -0.109375 to 0.109375
- output_weight: bfloat16 [4096, 2880], P('head'), may hold values from -0.09375 to 0.09375
- key_cache: bfloat16 [8, 8, 16, 65536], P('member', 'head'), may hold values from -330 to 330
- value_cache: bfloat16 [8, 8, 16, 65536], P('member', 'head'), may hold values from -8 to 8
- sink_logits: float32 [64], P('head'), may hold values from 3 to 10
- lengths: int32 [8, 16], P('member'), may hold values from 2 to 1024, as said below
- query_left: float32 [8, 4, 2880], P('member'), may hold values from -6 to 6
- query_right: float32 [8, 4, 4096], P('member', None, 'head'), may hold values from -6 to 6
- output_left: float32 [8, 4, 4096], P('member', None, 'head'), may hold values from -6 to 6
- output_right: float32 [8, 4, 2880], P('member'), may hold values from -6 to 6
- fitness: float32 [8], P('member'), may hold values from -4 to 4
- query_master: float32 [2880, 4096], P('member', 'head'), may hold values from -6 to 6
- query_moment: float32 [2880, 4096], P('member', 'head'), may hold values from -2 to 2
- output_master: float32 [2880, 4096], P('member', 'head'), may hold values from -6 to 6
- output_moment: float32 [2880, 4096], P('member', 'head'), may hold values from -2 to 2
Outputs:
- layer_output: bfloat16 [8, 32, 16, 2880], P('member', 'head')
- query_weights: float32 [2880, 4096], P('member', 'head')
- query_momenta: float32 [2880, 4096], P('member', 'head')
- output_weights: float32 [2880, 4096], P('member', 'head')
- output_momenta: float32 [2880, 4096], P('member', 'head')
The draws below stay inside these ranges and needn't reach their ends.
Inputs may be any that keep to these rules, and one draw needn't show every extreme that they name: `lengths`: in every member one sequence has all 1024 slots filled.
All inputs are finite; a program needn't handle non-finite values.
Results may differ from the reference program's by a relative error of at most 0.012.
Values may be sent and summed in bfloat16 or wider, within the bound.
A program may use at most 128 MiB of HBM per device.

```python
import math
import jax
import jax.numpy as jnp
from jax import lax

D = 2880
HEADS = 64
KV_HEADS = 8
HEAD_DIM = 64
RANK = 4
ROWS = 16
CACHE = 1024
STEPS = 32
GROUP = 8
QDIM = 4096
MEMBERS = 8


def draw_key_cache(key, part):
    full_shape = (MEMBERS, KV_HEADS, ROWS, CACHE, HEAD_DIM)
    first_key = jax.random.fold_in(jax.random.fold_in(key, 11), 0)
    base_keys = 1.5 * jax.random.truncated_normal(first_key, -4.0, 4.0, full_shape, jnp.float32)
    return base_keys.reshape(MEMBERS, KV_HEADS, ROWS, CACHE * HEAD_DIM).astype(jnp.bfloat16)


def draw_lengths(key, part):
    first_key, second_key = jax.random.split(jax.random.fold_in(key, 23))
    drawn = jax.random.randint(first_key, (MEMBERS, ROWS), 2, CACHE + 1)
    full_row = jax.random.randint(second_key, (MEMBERS, 1), 0, ROWS)
    row_ids = jnp.arange(ROWS, dtype=jnp.int32)[None, :]
    return jnp.where(row_ids == full_row, CACHE, drawn).astype(jnp.int32)


def levels(key, dims, shards, least, largest):
    factor_of = 1.0
    for position, blocks in shards:
        draws = jax.random.uniform(jax.random.fold_in(jax.random.fold_in(key, 6), position), (blocks,), jnp.float32, least / len(shards), largest / len(shards))
        factor_of = factor_of * jnp.repeat(jnp.exp(draws), dims[position] // blocks).reshape((-1,) + (1,) * (len(dims) - 1 - position))
    return factor_of


def scatter_about(rng, shape, scale, limit, pieces=(), held_as=jnp.bfloat16):
    values = jax.random.normal(rng, shape, jnp.float32) * scale
    if len(pieces) > 0:
        values = levels(rng, shape, pieces, -0.22, 0.18) * values
    return jnp.clip(values, min=-limit, max=limit).astype(held_as)


def setup_inputs(seed: int = 0) -> dict:
    splits = jax.random.split(jax.random.key(seed), 17)
    hidden = scatter_about(splits[0], (MEMBERS, STEPS, ROWS, D), 1.0, 6.0, ((0, 8), (1, 4)))
    joined_weight = scatter_about(splits[1], (D, KV_HEADS, (GROUP + 2) * HEAD_DIM), D ** -0.5, 0.109375, ((1, 4),))
    output_weight = scatter_about(splits[2], (QDIM, D), QDIM ** -0.5, 0.09375, ((0, 4),))
    key_cache = draw_key_cache(jax.random.fold_in(splits[16], 71), 0)
    value_cache = scatter_about(splits[4], (MEMBERS, KV_HEADS, ROWS, CACHE * HEAD_DIM), 2.0, 8.0, ((0, 8), (1, 4)))
    sink_logits = jnp.clip(3.0 + 7.0 * jax.random.uniform(splits[5], (HEADS,), jnp.float32) ** levels(splits[5], (HEADS,), ((0, 4),), -0.2, 0.2), 3.0, 10.0)
    lengths = draw_lengths(jax.random.fold_in(splits[16], 71), 0)
    query_left = scatter_about(splits[7], (MEMBERS, RANK, D), 1.0, 6.0, ((0, 8),), jnp.float32)
    query_right = scatter_about(splits[8], (MEMBERS, RANK, QDIM), 1.0, 6.0, ((0, 8), (2, 4)), jnp.float32)
    output_left = scatter_about(splits[9], (MEMBERS, RANK, QDIM), 1.0, 6.0, ((0, 8), (2, 4)), jnp.float32)
    output_right = scatter_about(splits[10], (MEMBERS, RANK, D), 1.0, 6.0, ((0, 8),), jnp.float32)
    fitness = scatter_about(splits[11], (MEMBERS,), 1.0, 4.0, ((0, 8),), jnp.float32)
    query_master = scatter_about(splits[12], (D, QDIM), 1.0, 6.0, ((0, 8), (1, 4)), jnp.float32)
    query_moment = scatter_about(splits[13], (D, QDIM), 0.3, 2.0, ((0, 8), (1, 4)), jnp.float32)
    output_master = scatter_about(splits[14], (D, QDIM), 1.0, 6.0, ((0, 8), (1, 4)), jnp.float32)
    output_moment = scatter_about(splits[15], (D, QDIM), 0.3, 2.0, ((0, 8), (1, 4)), jnp.float32)
    return dict(hidden=hidden, joined_weight=joined_weight, output_weight=output_weight, key_cache=key_cache, value_cache=value_cache, sink_logits=sink_logits, lengths=lengths, query_left=query_left, query_right=query_right, output_left=output_left, output_right=output_right, fitness=fitness, query_master=query_master, query_moment=query_moment, output_master=output_master, output_moment=output_moment)


rotary_base = 150000.0
noise_scale = 0.5
moment_decay = 0.9
learn_rate = 0.2
masked_score = -1e+30

def rotate(vectors, positions):
    half_dim = vectors.shape[-1] // 2
    exponents = jnp.arange(half_dim, dtype=jnp.float32) * (-2.0 / vectors.shape[-1])
    frequency = jnp.power(jnp.float32(rotary_base), exponents)
    angles = positions.astype(jnp.float32)[..., None] * frequency
    cosines = jnp.cos(angles)
    sine_part = jnp.sin(angles)
    first_half = vectors[..., :half_dim]
    second_half = vectors[..., half_dim:]
    return jnp.concatenate([first_half * cosines - second_half * sine_part, second_half * cosines + first_half * sine_part], axis=-1)

def attend(projected, member_lengths, member_keys, member_values, sink_values):
    step_count, row_count, kv_count, width, head_dim = projected.shape
    group = width - 2
    cache_len = member_keys.shape[-1] // head_dim
    positions = member_lengths[None, :] + jnp.arange(step_count, dtype=jnp.int32)[:, None]
    queries = rotate(projected[:, :, :, :group], positions[:, :, None, None]).astype(jnp.bfloat16)
    keys_new = rotate(projected[:, :, :, group], positions[:, :, None]).astype(jnp.bfloat16)
    values_new = projected[:, :, :, group + 1].astype(jnp.bfloat16)
    cache_keys = member_keys.reshape(kv_count, row_count, cache_len, head_dim)
    cache_values = member_values.reshape(kv_count, row_count, cache_len, head_dim)
    score_scale = head_dim ** (-0.5)
    cache_scores = jnp.einsum('sbjgd,jbtd->jbgst', queries.astype(jnp.float32), cache_keys.astype(jnp.float32)) * score_scale
    in_cache = jnp.arange(cache_len, dtype=jnp.int32)[None, :] < member_lengths[:, None]
    cache_scores = jnp.where(in_cache[None, :, None, None, :], cache_scores, masked_score)
    new_scores = jnp.einsum('sbjgd,ubjd->jbgsu', queries.astype(jnp.float32), keys_new.astype(jnp.float32)) * score_scale
    earlier = jnp.arange(step_count)[None, :] <= jnp.arange(step_count)[:, None]
    new_scores = jnp.where(earlier[None, None, None, :, :], new_scores, masked_score)
    sinks = sink_values.reshape(kv_count, 1, group, 1)
    maximum = jnp.maximum(jnp.maximum(cache_scores.max(-1), new_scores.max(-1)), sinks)
    cache_exp = jnp.exp(cache_scores - maximum[..., None])
    new_exp = jnp.exp(new_scores - maximum[..., None])
    denominator = cache_exp.sum(-1) + new_exp.sum(-1) + jnp.exp(sinks - maximum)
    cache_weights = (cache_exp / denominator[..., None]).astype(jnp.bfloat16)
    new_weights = (new_exp / denominator[..., None]).astype(jnp.bfloat16)
    attended = jnp.einsum('jbgst,jbtd->sbjgd', cache_weights.astype(jnp.float32), cache_values.astype(jnp.float32))
    attended = attended + jnp.einsum('jbgsu,ubjd->sbjgd', new_weights.astype(jnp.float32), values_new.astype(jnp.float32))
    return attended.astype(jnp.bfloat16).reshape(step_count, row_count, kv_count * group * head_dim)

def reference(hidden, joined_weight, output_weight, key_cache, value_cache, sink_logits, lengths, query_left, query_right, output_left, output_right, fitness, query_master, query_moment, output_master, output_moment):
    flat_weight = joined_weight.reshape(D, -1)

    def per_member(member_data):
        member_hidden, member_keys, member_values, member_lengths, left_q, right_q, left_o, right_o = member_data
        token_rows = member_hidden.reshape(STEPS * ROWS, D)
        projected = jnp.dot(token_rows, flat_weight, preferred_element_type=jnp.float32)
        projected = projected.reshape(STEPS * ROWS, KV_HEADS, GROUP + 2, HEAD_DIM)
        low_rank = jnp.dot(token_rows.astype(jnp.float32), left_q.T, precision=lax.Precision.HIGHEST)
        perturbed = jnp.dot(low_rank, right_q, precision=lax.Precision.HIGHEST) * (noise_scale / math.sqrt(D))
        query_part = projected[:, :, :GROUP] + perturbed.reshape(STEPS * ROWS, KV_HEADS, GROUP, HEAD_DIM)
        projected = jnp.concatenate([query_part, projected[:, :, GROUP:]], axis=2)
        projected = projected.reshape(STEPS, ROWS, KV_HEADS, GROUP + 2, HEAD_DIM)
        attended = attend(projected, member_lengths, member_keys, member_values, sink_logits)
        flat_attn = attended.reshape(STEPS * ROWS, QDIM)
        base_term = jnp.dot(flat_attn, output_weight, preferred_element_type=jnp.float32)
        low_out = jnp.dot(flat_attn.astype(jnp.float32), left_o.T, precision=lax.Precision.HIGHEST)
        extra_term = jnp.dot(low_out, right_o, precision=lax.Precision.HIGHEST) * (noise_scale / math.sqrt(QDIM))
        return (base_term + extra_term).astype(jnp.bfloat16).reshape(STEPS, ROWS, D)
    layer_output = lax.map(per_member, (hidden, key_cache, value_cache, lengths, query_left, query_right, output_left, output_right))
    weighted_query = query_right * fitness[:, None, None]
    weighted_output = output_left * fitness[:, None, None]
    query_step = jnp.einsum('mkd,mkc->dc', query_left, weighted_query, precision=lax.Precision.HIGHEST) / MEMBERS
    output_step = jnp.einsum('mkd,mkc->dc', output_right, weighted_output, precision=lax.Precision.HIGHEST) / MEMBERS
    query_momenta = moment_decay * query_moment + query_step
    output_momenta = moment_decay * output_moment + output_step
    query_weights = query_master + learn_rate * query_momenta
    output_weights = output_master + learn_rate * output_momenta
    return (layer_output, query_weights, query_momenta, output_weights, output_momenta)
```

```python
import functools
import math

import jax
import jax.numpy as jnp
from jax import lax
from jax.experimental import pallas as pl
from jax.experimental.pallas import tpu as pltpu
from jax.sharding import PartitionSpec as P

HEAD_DIM = 64
SHARES = (2, 4, 4)
CHUNKS = 4
VMEM_LIMIT = 58 * 1024 * 1024

rotary_base = 150000.0
noise_scale = 0.5
moment_decay = 0.9
learn_rate = 0.2
masked_score = -1e30
LOG2E = 1.4426950408889634


def attend_kernel(first_row, parts, len_ref, proj_ref, key_ref, value_ref, cos_ref, sin_ref, sink_ref, late_ref, out_ref):
    filled = len_ref[first_row + pl.program_id(0)]
    lead, _, inner, width = proj_ref.shape
    steps = lead * inner
    pairs = (width // 128) - 1
    slots2 = key_ref.shape[2]
    part = slots2 // parts
    x = proj_ref[...].reshape(steps, width)
    cosines = cos_ref[0]
    sines = sin_ref[0]
    lane = lax.broadcasted_iota(jnp.int32, (steps, 128), 1)
    low = lane < 64
    first = (lane & 63) < 32
    score_scale = HEAD_DIM ** (-0.5) * LOG2E

    def rotated(block):
        swapped = jnp.where(first, pltpu.roll(block, 96, 1), pltpu.roll(block, 32, 1))
        return block * cosines + swapped * sines

    even_rows, odd_rows = [], []
    zero = jnp.zeros((steps, 128), jnp.float32)
    for i in range(pairs):
        turned = rotated(x[:, 128 * i : 128 * i + 128]) * score_scale
        other = pltpu.roll(turned, 64, 1)
        even_rows += [jnp.where(low, turned, zero), jnp.where(low, other, zero)]
        odd_rows += [jnp.where(low, zero, other), jnp.where(low, zero, turned)]
    query_even = jnp.concatenate(even_rows, axis=0).astype(jnp.bfloat16)
    query_odd = jnp.concatenate(odd_rows, axis=0).astype(jnp.bfloat16)
    pair = x[:, 128 * pairs :]
    fresh = jnp.where(low, rotated(pair), pair).astype(jnp.bfloat16)
    rows = query_even.shape[0]
    transposed = (((1,), (1,)), ((), ()))
    new_scores = lax.dot_general(query_even, fresh, transposed, preferred_element_type=jnp.float32)
    new_scores = new_scores + late_ref[...]
    sink = sink_ref[0][:, :1]
    used = (filled + (2 * part - 1)) // (2 * part)
    one = jnp.ones((), jnp.bfloat16)
    fresh_odd = jnp.where(low, one, fresh)

    for count in range(1, parts + 1):

        @pl.when(used == count)
        def _():
            span = count * part
            keys = key_ref[0, 0, :span, :]
            values = value_ref[0, 0, :span, :]
            low_lane = lax.broadcasted_iota(jnp.int32, (span, 128), 1) < 64
            even = lax.dot_general(query_even, keys, transposed, preferred_element_type=jnp.float32)
            odd = lax.dot_general(query_odd, keys, transposed, preferred_element_type=jnp.float32)
            slot = 2 * (lax.broadcasted_iota(jnp.int32, (rows, part), 1) + (span - part))

            def masked(scores, offset):
                last = jnp.where(slot + offset < filled, scores[:, span - part :], masked_score)
                return jnp.concatenate([scores[:, : span - part], last], axis=1) if count > 1 else last

            even = masked(even, 0)
            odd = masked(odd, 1)
            top = jnp.max(jnp.maximum(even, odd), axis=1, keepdims=True)
            top = jnp.maximum(top, jnp.max(new_scores, axis=1, keepdims=True))
            top = jnp.maximum(top, sink)
            even = jnp.exp2(even - top).astype(jnp.bfloat16)
            odd = jnp.exp2(odd - top).astype(jnp.bfloat16)
            new = jnp.exp2(new_scores - top).astype(jnp.bfloat16)
            from_even = jnp.dot(even, jnp.where(low_lane, values, one), preferred_element_type=jnp.float32)
            from_odd = jnp.dot(odd, jnp.where(low_lane, one, values), preferred_element_type=jnp.float32)
            from_odd = from_odd + jnp.dot(new, fresh_odd, preferred_element_type=jnp.float32)
            mixed = from_even + pltpu.roll(from_odd, 64, 1)
            swapped = pltpu.roll(mixed, 64, 1)
            sink_part = jnp.exp2(sink - top)
            for i in range(pairs):
                left = slice(2 * i * steps, (2 * i + 1) * steps)
                right = slice((2 * i + 1) * steps, (2 * i + 2) * steps)
                upper = jnp.where(low, mixed[left], swapped[right])
                total = jnp.where(
                    low, swapped[left] + sink_part[left], mixed[right] + sink_part[right]
                )
                out_ref[:, 0, :, 128 * i : 128 * i + 128] = (
                    (upper / total).reshape(lead, inner, 128).astype(out_ref.dtype)
                )


def attend(first_row, projected, lengths, keys, values, cosines, sines, sinks, late, kv_count):
    lead, row_count, inner, width = projected.shape
    kv_width = width // kv_count
    out_width = kv_width - 2 * HEAD_DIM
    slots2 = keys.shape[2]
    parts = 4 if slots2 % 512 == 0 else 1
    grid_spec = pltpu.PrefetchScalarGridSpec(
        num_scalar_prefetch=1,
        grid=(row_count, kv_count),
        in_specs=[
            pl.BlockSpec((lead, 1, inner, kv_width), lambda b, j, n: (0, b, 0, j)),
            pl.BlockSpec((1, 1, slots2, 128), lambda b, j, n: (j, b + first_row, 0, 0)),
            pl.BlockSpec((1, 1, slots2, 128), lambda b, j, n: (j, b + first_row, 0, 0)),
            pl.BlockSpec((1, lead * inner, 128), lambda b, j, n: (b + first_row, 0, 0)),
            pl.BlockSpec((1, lead * inner, 128), lambda b, j, n: (b + first_row, 0, 0)),
            pl.BlockSpec((1,) + sinks.shape[1:], lambda b, j, n: (j, 0, 0)),
            pl.BlockSpec(late.shape, lambda b, j, n: (0, 0)),
        ],
        out_specs=pl.BlockSpec((lead, 1, inner, out_width), lambda b, j, n: (0, b, 0, j)),
    )
    return pl.pallas_call(
        functools.partial(attend_kernel, first_row, parts),
        grid_spec=grid_spec,
        out_shape=jax.ShapeDtypeStruct((lead, row_count, inner, kv_count * out_width), jnp.bfloat16),
        compiler_params=pltpu.CompilerParams(vmem_limit_bytes=32 * 1024 * 1024),
        cost_estimate=pl.CostEstimate(
            flops=row_count * kv_count * 2 * 2 * 512 * 512 * 128,
            bytes_accessed=row_count * kv_count * slots2 * 512,
            transcendentals=row_count * kv_count * 256 * 1024,
        ),
    )(lengths, projected, keys, values, cosines, sines, sinks, late)


def split(values):
    high = values.astype(jnp.bfloat16)
    return high, (values - high.astype(jnp.float32)).astype(jnp.bfloat16)


def outer_sum(left, right):
    left_high, left_low = split(left)
    right_high, right_low = split(right)
    return lax.dot_general(
        jnp.concatenate([left_high, left_high, left_low], axis=0),
        jnp.concatenate([right_high, right_low, right_high], axis=0),
        (((0,), (0,)), ((), ())),
        preferred_element_type=jnp.float32,
    )


def crossed(block, axis, mask):
    count = lax.axis_size(axis)
    return lax.ppermute(block, axis, [(i, i ^ mask) for i in range(count)])


def first_blocks(own, heads):
    blocks = {m: crossed(own, "head", m) for m in range(1, heads) if m == 1 or m % 2 == 0}
    return {0: own, **blocks}


def first_hop(partial, heads):
    passed = []
    for m in range(2, heads, 2):
        extra = crossed(partial[m + 1], "head", 1).astype(jnp.float32)
        passed.append((partial[m].astype(jnp.float32) + extra).astype(jnp.bfloat16))
    return partial[0], partial[1], passed


def second_hop(own, near, passed):
    received = [crossed(block, "head", 2 * i + 2) for i, block in enumerate(passed)]
    return own, [crossed(near, "head", 1)] + received


def total_of(own, received):
    return sum([block.astype(jnp.float32) for block in received], own.astype(jnp.float32)).astype(
        jnp.bfloat16
    )


def shards(
    hidden,
    joined_weight,
    output_weight,
    key_cache,
    value_cache,
    sink_logits,
    lengths,
    query_left,
    query_right,
    output_left,
    output_right,
    fitness,
    query_master,
    query_moment,
    output_master,
    output_moment,
):
    model, kv_count, kv_width = joined_weight.shape
    group = kv_width // HEAD_DIM - 2
    q_width = group * HEAD_DIM
    heads = lax.axis_size("head")
    members = lax.axis_size("member")
    _, own_steps, row_count, _ = hidden.shape
    steps = heads * own_steps
    feature_count = heads * output_weight.shape[0]
    query_scale = noise_scale / math.sqrt(model)
    output_scale = noise_scale / math.sqrt(feature_count)
    bounds = [0]
    for share in SHARES:
        bounds.append(bounds[-1] + row_count // share)

    local = hidden[0].transpose(1, 0, 2)
    first_landed = first_blocks(local[: bounds[1]], heads)

    def gather_rest(landed):
        gathered = []
        for first_row, end_row in zip(bounds[1:], bounds[2:] + [None]):
            blocks = dict(landed)
            for m in range(3, heads, 2):
                blocks[m] = crossed(blocks[m - 1], "head", 1)
            gathered.append(jnp.stack([blocks[m] for m in range(heads)]))
            if end_row is not None:
                own, _ = lax.optimization_barrier((local[first_row:end_row], landed))
                landed = first_blocks(own, heads)
        return gathered

    factors = jnp.concatenate(
        [query_left, output_right, query_right * fitness[0], output_left * fitness[0]], axis=2
    ).astype(jnp.bfloat16)
    every, distance = factors[0], 1
    if members & (members - 1):
        every = lax.all_gather(every, "member", axis=0, tiled=True)
        distance = members

    right_padded = jnp.pad(
        (query_right[0] * query_scale).reshape(-1, kv_count, q_width),
        ((0, 0), (0, 0), (0, kv_width - q_width)),
    ).reshape(-1, kv_count * kv_width)
    flat_weight = joined_weight.reshape(model, kv_count * kv_width)
    out_factor = output_right[0] * output_scale
    pair_count = key_cache.shape[-1] // 128
    keys = key_cache[0].reshape(kv_count, row_count, pair_count, 128)
    values = value_cache[0].reshape(kv_count, row_count, pair_count, 128)
    flat_weight, keys, values, out_factor, first_landed = lax.optimization_barrier(
        (flat_weight, keys, values, out_factor, first_landed)
    )
    gathered = gather_rest(first_landed)
    in_weight = (flat_weight.astype(jnp.float32) + outer_sum(query_left[0], right_padded)).astype(
        jnp.bfloat16
    )
    out_weight = (
        output_weight.T.astype(jnp.float32)
        + outer_sum(out_factor, output_left[0])
    ).astype(jnp.bfloat16)

    half_dim = HEAD_DIM // 2
    exponents = jnp.arange(half_dim, dtype=jnp.float32) * (-2.0 / HEAD_DIM)
    frequency = jnp.power(jnp.float32(rotary_base), exponents)
    owners = lax.axis_index("head") ^ jnp.arange(heads, dtype=jnp.int32)
    step_ids = (owners[:, None] * own_steps + jnp.arange(own_steps, dtype=jnp.int32)).reshape(-1)
    positions = lengths[0][:, None] + step_ids[None, :]
    angles = positions.astype(jnp.float32)[..., None] * frequency
    cosines = jnp.cos(angles)
    sines = jnp.sin(angles)
    cosines = jnp.concatenate([cosines, cosines, cosines, cosines], axis=-1)
    sines = jnp.concatenate([-sines, sines, -sines, sines], axis=-1)
    late = jnp.where(step_ids[None, :] <= step_ids[:, None], 0.0, masked_score)
    late = jnp.broadcast_to(late[None], (group, steps, steps)).reshape(group * steps, steps)
    late = late.astype(jnp.float32)
    sinks = jnp.broadcast_to(
        (sink_logits * LOG2E).reshape(kv_count, group, 1, 1), (kv_count, group, steps, 128)
    ).reshape(kv_count, group * steps, 128)

    pieces = []
    partial, hopped = None, None
    for c, (first_row, end_row) in enumerate(zip(bounds[:-1], bounds[1:])):
        chunk = end_row - first_row
        token_rows = gathered[c].reshape(-1, model)
        if partial is not None:
            token_rows, partial = lax.optimization_barrier((token_rows, partial))
        projected = jnp.dot(token_rows, in_weight, preferred_element_type=jnp.float32)
        projected = projected.reshape(heads, chunk, own_steps, kv_count * kv_width)
        if own_steps % 8:
            projected = projected.transpose(1, 0, 2, 3).reshape(1, chunk, steps, kv_count * kv_width)
        attended = attend(
            first_row, projected, lengths[0], keys, values, cosines, sines, sinks, late, kv_count
        )
        landed = None if hopped is None else second_hop(*hopped)
        hopped = None if partial is None else first_hop(partial, heads)
        if distance < members:
            every = jnp.concatenate([every, crossed(every, "member", distance)], axis=0)
            distance *= 2
        attended, landed, hopped, every = lax.optimization_barrier((attended, landed, hopped, every))
        if landed is not None:
            pieces.append(total_of(*landed).reshape(-1, own_steps, model))
        flat = attended
        if own_steps % 8:
            flat = attended.reshape(chunk, heads, own_steps, -1).transpose(1, 0, 2, 3)
        flat = flat.reshape(heads * chunk * own_steps, -1)
        partial = lax.dot_general(
            flat, out_weight, (((1,), (1,)), ((), ())), preferred_element_type=jnp.float32
        ).astype(jnp.bfloat16)
        partial = partial.reshape(heads, chunk * own_steps, model)
    landed = second_hop(*hopped)
    pieces.append(total_of(*landed).reshape(-1, own_steps, model))
    landed = second_hop(*first_hop(partial, heads))
    pieces.append(total_of(*landed).reshape(-1, own_steps, model))
    layer_output = jnp.concatenate(pieces, axis=0).transpose(1, 0, 2)[None]

    while distance < members:
        every = jnp.concatenate([every, crossed(every, "member", distance)], axis=0)
        distance *= 2
    row_share, columns = query_master.shape
    row_start = lax.axis_index("member") * row_share
    left_query = lax.dynamic_slice_in_dim(every, row_start, row_share, 1)
    left_output = lax.dynamic_slice_in_dim(every, model + row_start, row_share, 1)
    right_query = every[:, 2 * model : 2 * model + columns]
    right_output = every[:, 2 * model + columns :]

    def stepped(left, right):
        total = lax.dot_general(
            left, right, (((0,), (0,)), ((), ())), preferred_element_type=jnp.float32
        )
        return total / members

    query_momenta = moment_decay * query_moment + stepped(left_query, right_query)
    output_momenta = moment_decay * output_moment + stepped(left_output, right_output)
    query_weights = query_master + learn_rate * query_momenta
    output_weights = output_master + learn_rate * output_momenta
    return (layer_output, query_weights, query_momenta, output_weights, output_momenta)


def layer_kernel(
    heads,
    members,
    chunks,
    kv_count,
    own_ref,
    weight_ref,
    left_ref,
    right_ref,
    key_ref,
    value_ref,
    bias_ref,
    cos_ref,
    sin_ref,
    sink_ref,
    late_ref,
    out_weight_ref,
    out_left_ref,
    out_right_ref,
    factor_ref,
    out_ref,
    every_ref,
    gathered,
    partial,
    from_left,
    from_right,
    projected,
    attended,
    own_sem,
    gather_sem,
    right_sem,
    left_sem,
    sum_right_sem,
    sum_left_sem,
    right_sum_sem,
    left_sum_sem,
    factor_send,
    factor_recv,
):
    me = lax.axis_index("head")
    mine = lax.axis_index("member")
    last = heads - 1
    rows = own_ref.shape[0] // chunks
    inner = projected.shape[1] * chunks // key_ref.shape[1]
    row_count = rows // inner
    width = projected.shape[2] // kv_count
    pairs = width // 128 - 1
    out_width = pairs * 128
    steps = heads * inner
    right = {"head": jnp.minimum(me + 1, last)}
    left = {"head": jnp.maximum(me - 1, 0)}
    mesh_id = pl.DeviceIdType.MESH

    barrier = pltpu.get_barrier_semaphore()

    @pl.when(me > 0)
    def _():
        pl.semaphore_signal(barrier, inc=1, device_id=left, device_id_type=mesh_id)

    @pl.when(me < last)
    def _():
        pl.semaphore_signal(barrier, inc=1, device_id=right, device_id_type=mesh_id)

    def peer(o):
        return {"member": lax.rem(mine + o, members)}

    for o in range(1, members):
        pl.semaphore_signal(barrier, inc=1, device_id=peer(o), device_id_type=mesh_id)
    neighbours = jnp.where(me > 0, 1, 0) + jnp.where(me < last, 1, 0) + (members - 1)
    pl.semaphore_wait(barrier, neighbours)

    def push(source, target, send, receive, device):
        return pltpu.make_async_remote_copy(
            src_ref=source,
            dst_ref=target,
            send_sem=send,
            recv_sem=receive,
            device_id=device,
            device_id_type=mesh_id,
        )

    def span(c):
        return pl.ds(c * rows, rows)

    def own_copy(c, send, device):
        return push(
            own_ref.at[span(c)], gathered.at[me, span(c)], send.at[me, c], gather_sem.at[me, c], device
        )

    def block_copy(k, c, send, device):
        block = gathered.at[k, span(c)]
        return push(block, block, send.at[k, c], gather_sem.at[k, c], device)

    def send_own(c):
        @pl.when(me < last)
        def _():
            own_copy(c, right_sem, right).start()

        @pl.when(me > 0)
        def _():
            own_copy(c, left_sem, left).start()

    def forward(t, c):
        k = jnp.maximum(me - t, 0)

        @pl.when((me >= t) & (me < last))
        def _():
            block_copy(k, c, right_sem, right).wait_recv()
            block_copy(k, c, right_sem, right).start()

        n = jnp.minimum(me + t, last)

        @pl.when((me + t <= last) & (me > 0))
        def _():
            block_copy(n, c, left_sem, left).wait_recv()
            block_copy(n, c, left_sem, left).start()

    def land(c):
        for t in range(1, heads):

            @pl.when((me == last) & (me >= t))
            def _():
                block_copy(jnp.maximum(me - t, 0), c, right_sem, right).wait_recv()

            @pl.when((me == 0) & (me + t <= last))
            def _():
                block_copy(jnp.minimum(me + t, last), c, left_sem, left).wait_recv()

    def right_sum(d, c):
        return push(
            partial.at[d, span(c)],
            from_left.at[d, span(c)],
            sum_right_sem.at[d, c],
            right_sum_sem.at[d, c],
            right,
        )

    def left_sum(d, c):
        return push(
            partial.at[d, span(c)],
            from_right.at[d, span(c)],
            sum_left_sem.at[d, c],
            left_sum_sem.at[d, c],
            left,
        )

    def add_in(d, c, landed):
        total = partial[d, span(c)].astype(jnp.float32) + landed[d, span(c)].astype(jnp.float32)
        partial[d, span(c)] = total.astype(partial.dtype)

    def sum_first(c):
        @pl.when(me == 0)
        def _():
            for d in range(last, 0, -1):
                right_sum(d, c).start()

        @pl.when(me == last)
        def _():
            for d in range(last):
                left_sum(d, c).start()

    def sum_next(c):
        for t in range(last):
            d = last - t

            @pl.when((me > 0) & (me < d))
            def _():
                right_sum(d, c).wait_recv()
                add_in(d, c, from_left)
                right_sum(d, c).start()

            @pl.when((me < last) & (me > t))
            def _():
                left_sum(t, c).wait_recv()
                add_in(t, c, from_right)
                left_sum(t, c).start()

    def sum_last(c):
        total = partial[me, span(c)].astype(jnp.float32)

        @pl.when(me > 0)
        def _():
            right_sum(me, c).wait_recv()

        @pl.when(me < last)
        def _():
            left_sum(me, c).wait_recv()

        @pl.when((me > 0) & (me < last))
        def _():
            both = from_left[me, span(c)].astype(jnp.float32)
            both = both + from_right[me, span(c)].astype(jnp.float32)
            out_ref[span(c)] = (total + both).astype(out_ref.dtype)

        @pl.when(me == 0)
        def _():
            out_ref[span(c)] = (total + from_right[me, span(c)].astype(jnp.float32)).astype(out_ref.dtype)

        @pl.when(me == last)
        def _():
            out_ref[span(c)] = (total + from_left[me, span(c)].astype(jnp.float32)).astype(out_ref.dtype)

    def factor_copy(o):
        return push(factor_ref, every_ref.at[mine], factor_send.at[o], factor_recv.at[o], peer(o))

    send_own(0)
    if chunks > 1:
        send_own(1)
    for o in range(1, members):
        factor_copy(o).start()
    every_ref[mine] = factor_ref[...]
    keep = pltpu.make_async_copy(own_ref, gathered.at[me], own_sem)
    keep.start()

    lane = lax.broadcasted_iota(jnp.int32, (steps, 128), 1)
    low = lane < HEAD_DIM
    first = (lane & (HEAD_DIM - 1)) < HEAD_DIM // 2
    score_scale = HEAD_DIM ** (-0.5) * LOG2E
    transposed = (((1,), (1,)), ((), ()))
    one = jnp.ones((), jnp.bfloat16)

    def project(c):
        x = gathered[:, span(c), :].reshape(heads * rows, -1)
        thin = lax.dot_general(x, left_ref[...], transposed, preferred_element_type=jnp.float32)
        thin = thin.astype(jnp.bfloat16)
        for j in range(kv_count):
            columns = slice(j * width, (j + 1) * width)
            tile = jnp.dot(x, weight_ref[:, columns], preferred_element_type=jnp.float32)
            tile = tile + jnp.dot(thin, right_ref[:, columns], preferred_element_type=jnp.float32)
            projected[:, :, columns] = tile.reshape(heads, rows, width)

    def attend_one(b, s, j):
        place = pl.ds(pl.multiple_of(s * inner, inner), inner)
        x = projected[:, place, j * width : (j + 1) * width].reshape(steps, width)
        cosines = cos_ref[b]
        sines = sin_ref[b]

        def rotated(block):
            swapped = jnp.where(first, pltpu.roll(block, 96, 1), pltpu.roll(block, 32, 1))
            return block * cosines + swapped * sines

        even_rows, odd_rows = [], []
        zero = jnp.zeros((steps, 128), jnp.float32)
        for i in range(pairs):
            turned = rotated(x[:, 128 * i : 128 * i + 128]) * score_scale
            other = pltpu.roll(turned, 64, 1)
            even_rows += [jnp.where(low, turned, zero), jnp.where(low, other, zero)]
            odd_rows += [jnp.where(low, zero, other), jnp.where(low, zero, turned)]
        query_even = jnp.concatenate(even_rows, axis=0).astype(jnp.bfloat16)
        query_odd = jnp.concatenate(odd_rows, axis=0).astype(jnp.bfloat16)
        pair = x[:, 128 * pairs :]
        fresh = jnp.where(low, rotated(pair), pair).astype(jnp.bfloat16)
        new_scores = lax.dot_general(query_even, fresh, transposed, preferred_element_type=jnp.float32)
        new_scores = new_scores + late_ref[...]
        sink = sink_ref[j][:, :1]
        fresh_odd = jnp.where(low, one, fresh)
        keys = key_ref[j, b]
        values = value_ref[j, b]
        bias = bias_ref[b]
        low_lane = lax.broadcasted_iota(jnp.int32, values.shape, 1) < HEAD_DIM
        even = lax.dot_general(query_even, keys, transposed, preferred_element_type=jnp.float32)
        odd = lax.dot_general(query_odd, keys, transposed, preferred_element_type=jnp.float32)
        even = even + bias[0:1]
        odd = odd + bias[1:2]
        top = jnp.max(jnp.maximum(even, odd), axis=1, keepdims=True)
        top = jnp.maximum(top, jnp.max(new_scores, axis=1, keepdims=True))
        top = jnp.maximum(top, sink)
        even = jnp.exp2(even - top).astype(jnp.bfloat16)
        odd = jnp.exp2(odd - top).astype(jnp.bfloat16)
        new = jnp.exp2(new_scores - top).astype(jnp.bfloat16)
        from_even = jnp.dot(even, jnp.where(low_lane, values, one), preferred_element_type=jnp.float32)
        from_odd = jnp.dot(odd, jnp.where(low_lane, one, values), preferred_element_type=jnp.float32)
        from_odd = from_odd + jnp.dot(new, fresh_odd, preferred_element_type=jnp.float32)
        mixed = from_even + pltpu.roll(from_odd, 64, 1)
        swapped = pltpu.roll(mixed, 64, 1)
        sink_part = jnp.exp2(sink - top)
        for i in range(pairs):
            near = slice(2 * i * steps, (2 * i + 1) * steps)
            far = slice((2 * i + 1) * steps, (2 * i + 2) * steps)
            upper = jnp.where(low, mixed[near], swapped[far])
            total = jnp.where(low, swapped[near] + sink_part[near], mixed[far] + sink_part[far])
            start = j * out_width + 128 * i
            attended[:, place, start : start + 128] = (upper / total).reshape(heads, inner, 128)

    def put_out(c):
        x = attended[...].reshape(heads * rows, -1).astype(jnp.bfloat16)
        thin = lax.dot_general(x, out_left_ref[...], transposed, preferred_element_type=jnp.float32)
        thin = thin.astype(jnp.bfloat16)
        model = out_weight_ref.shape[0]
        for start in range(0, model, 768):
            columns = slice(start, min(start + 768, model))
            tile = lax.dot_general(
                x, out_weight_ref[columns], transposed, preferred_element_type=jnp.float32
            )
            tile = tile + jnp.dot(thin, out_right_ref[:, columns], preferred_element_type=jnp.float32)
            partial[:, span(c), columns] = tile.astype(partial.dtype).reshape(heads, rows, -1)

    keep.wait()
    for c in range(chunks):
        if c == 0:
            for t in range(1, heads):
                forward(t, c)
        land(c)
        project(c)
        if c + 2 < chunks:
            send_own(c + 2)

        def attend_rows(s, carry):
            for j in range(kv_count):
                attend_one(c * row_count + s, s, j)
            if c + 1 < chunks:
                for t in range(1, heads):

                    @pl.when(s == min(t * row_count // (heads - 1), row_count) - 1)
                    def _():
                        forward(t, c + 1)
            if c > 0:

                @pl.when(s == row_count // 2)
                def _():
                    sum_next(c - 1)

            return carry

        lax.fori_loop(0, row_count, attend_rows, 0)
        put_out(c)
        sum_first(c)
        if c > 0:
            sum_last(c - 1)
    sum_next(chunks - 1)
    for o in range(1, members):
        factor_copy(o).wait_recv()
    sum_last(chunks - 1)

    for o in range(1, members):
        factor_copy(o).wait_send()
    for c in range(chunks):

        @pl.when(me < last)
        def _():
            own_copy(c, right_sem, right).wait_send()

        @pl.when(me > 0)
        def _():
            own_copy(c, left_sem, left).wait_send()

        for k in range(heads):

            @pl.when((k < me) & (me < last))
            def _():
                block_copy(k, c, right_sem, right).wait_send()

            @pl.when((k > me) & (me > 0))
            def _():
                block_copy(k, c, left_sem, left).wait_send()

            @pl.when(k > me)
            def _():
                right_sum(k, c).wait_send()

            @pl.when(k < me)
            def _():
                left_sum(k, c).wait_send()


def whole_layer(operands, heads, members, chunks, kv_count, row_count):
    own, weight, right_columns = operands[0], operands[1], operands[1].shape[1]
    tokens, model = own.shape
    features = operands[11].shape[1]
    rows = tokens // chunks
    factor = operands[14]
    spec = pl.BlockSpec(memory_space=pltpu.VMEM)
    dma = pltpu.SemaphoreType.DMA
    return pl.pallas_call(
        functools.partial(layer_kernel, heads, members, chunks, kv_count),
        in_specs=[spec] * len(operands),
        out_specs=[spec, spec],
        out_shape=[
            jax.ShapeDtypeStruct((tokens, model), jnp.bfloat16),
            jax.ShapeDtypeStruct((members,) + factor.shape, jnp.bfloat16),
        ],
        scratch_shapes=[
            pltpu.VMEM((heads, tokens, model), jnp.bfloat16),
            pltpu.VMEM((heads, tokens, model), jnp.bfloat16),
            pltpu.VMEM((heads, tokens, model), jnp.bfloat16),
            pltpu.VMEM((heads, tokens, model), jnp.bfloat16),
            pltpu.VMEM((heads, rows, right_columns), jnp.float32),
            pltpu.VMEM((heads, rows, features), jnp.float32),
            dma,
            dma((heads, chunks)),
            dma((heads, chunks)),
            dma((heads, chunks)),
            dma((heads, chunks)),
            dma((heads, chunks)),
            dma((heads, chunks)),
            dma((heads, chunks)),
            dma((members,)),
            dma((members,)),
        ],
        compiler_params=pltpu.CompilerParams(
            collective_id=0, has_side_effects=True, vmem_limit_bytes=VMEM_LIMIT
        ),
    )(*operands)


def fused_shards(
    hidden,
    joined_weight,
    output_weight,
    key_cache,
    value_cache,
    sink_logits,
    lengths,
    query_left,
    query_right,
    output_left,
    output_right,
    fitness,
    query_master,
    query_moment,
    output_master,
    output_moment,
):
    model, kv_count, kv_width = joined_weight.shape
    group = kv_width // HEAD_DIM - 2
    q_width = group * HEAD_DIM
    heads = lax.axis_size("head")
    members = lax.axis_size("member")
    _, own_steps, row_count, _ = hidden.shape
    steps = heads * own_steps
    feature_count = heads * output_weight.shape[0]
    query_scale = noise_scale / math.sqrt(model)
    output_scale = noise_scale / math.sqrt(feature_count)
    own = hidden[0].transpose(1, 0, 2).reshape(row_count * own_steps, model)
    factors = jnp.concatenate(
        [query_left, output_right, query_right * fitness[0], output_left * fitness[0]], axis=2
    ).astype(jnp.bfloat16)

    def doubled(values):
        return jnp.concatenate([values, values], axis=0).astype(jnp.bfloat16)

    def padded(values):
        rank = values.shape[0]
        return jnp.pad(values, ((0, -rank % 8), (0, 0)))

    right_columns = jnp.pad(
        (query_right[0] * query_scale).reshape(-1, kv_count, q_width),
        ((0, 0), (0, 0), (0, kv_width - q_width)),
    ).reshape(-1, kv_count * kv_width)
    in_left = doubled(padded(query_left[0]))
    in_right = jnp.concatenate(split(padded(right_columns)), axis=0)
    out_left = doubled(padded(output_left[0]))
    out_right = jnp.concatenate(split(padded(output_right[0] * output_scale)), axis=0)
    flat_weight = joined_weight.reshape(model, kv_count * kv_width)
    pair_count = key_cache.shape[-1] // 128
    keys = key_cache[0].reshape(kv_count, row_count, pair_count, 128)
    values = value_cache[0].reshape(kv_count, row_count, pair_count, 128)
    slots = jnp.arange(2 * pair_count, dtype=jnp.int32).reshape(pair_count, 2).T
    bias = jnp.where(slots[None] < lengths[0][:, None, None], 0.0, masked_score).astype(jnp.float32)

    half_dim = HEAD_DIM // 2
    exponents = jnp.arange(half_dim, dtype=jnp.float32) * (-2.0 / HEAD_DIM)
    frequency = jnp.power(jnp.float32(rotary_base), exponents)
    step_ids = jnp.arange(steps, dtype=jnp.int32)
    positions = lengths[0][:, None] + step_ids[None, :]
    angles = positions.astype(jnp.float32)[..., None] * frequency
    cosines = jnp.cos(angles)
    sines = jnp.sin(angles)
    cosines = jnp.concatenate([cosines, cosines, cosines, cosines], axis=-1)
    sines = jnp.concatenate([-sines, sines, -sines, sines], axis=-1)
    late = jnp.where(step_ids[None, :] <= step_ids[:, None], 0.0, masked_score)
    late = jnp.broadcast_to(late[None], (group, steps, steps)).reshape(group * steps, steps)
    late = late.astype(jnp.float32)
    sinks = jnp.broadcast_to(
        (sink_logits * LOG2E).reshape(kv_count, group, 1, 1), (kv_count, group, steps, 128)
    ).reshape(kv_count, group * steps, 128)

    chunks = CHUNKS if row_count % CHUNKS == 0 else 1
    operands = [
        own, flat_weight, in_left, in_right, keys, values, bias, cosines, sines, sinks, late,
        output_weight.T, out_left, out_right, factors[0],
    ]
    layer_rows, every = whole_layer(operands, heads, members, chunks, kv_count, row_count)
    layer_output = layer_rows.reshape(row_count, own_steps, model).transpose(1, 0, 2)[None]
    every = every.reshape(-1, every.shape[-1])

    row_share, columns = query_master.shape
    row_start = lax.axis_index("member") * row_share
    left_query = lax.dynamic_slice_in_dim(every, row_start, row_share, 1)
    left_output = lax.dynamic_slice_in_dim(every, model + row_start, row_share, 1)
    right_query = every[:, 2 * model : 2 * model + columns]
    right_output = every[:, 2 * model + columns :]

    def stepped(left, right):
        total = lax.dot_general(
            left, right, (((0,), (0,)), ((), ())), preferred_element_type=jnp.float32
        )
        return total / members

    query_momenta = moment_decay * query_moment + stepped(left_query, right_query)
    output_momenta = moment_decay * output_moment + stepped(left_output, right_output)
    query_weights = query_master + learn_rate * query_momenta
    output_weights = output_master + learn_rate * output_momenta
    return (layer_output, query_weights, query_momenta, output_weights, output_momenta)


def layer(hidden, *others):
    body = fused_shards if hidden.shape[1] % 8 == 0 else shards
    return body(hidden, *others)


def solution(mesh):
    placed = (
        P("member", "head", None, None),
        P(None, "head", None),
        P("head", None),
        P("member", "head", None, None),
        P("member", "head", None, None),
        P("head"),
        P("member", None),
        P("member", None, None),
        P("member", None, "head"),
        P("member", None, "head"),
        P("member", None, None),
        P("member"),
        P("member", "head"),
        P("member", "head"),
        P("member", "head"),
        P("member", "head"),
    )
    return jax.shard_map(
        layer,
        mesh=mesh,
        in_specs=placed,
        out_specs=(
            P("member", "head", None, None),
            P("member", "head"),
            P("member", "head"),
            P("member", "head"),
            P("member", "head"),
        ),
        check_vma=False,
    )
```

```python
import functools
import math

import jax
import jax.numpy as jnp
from jax import lax
from jax.experimental import pallas as pl
from jax.experimental.pallas import tpu as pltpu
from jax.sharding import PartitionSpec as P

HEAD_DIM = 64
SHARES = (2, 4, 4)
SIZES = (4, 4, 4, 2, 2)
VMEM_LIMIT = 58 * 1024 * 1024

rotary_base = 150000.0
noise_scale = 0.5
moment_decay = 0.9
learn_rate = 0.2
masked_score = -1e30
LOG2E = 1.4426950408889634


def attend_kernel(first_row, parts, len_ref, proj_ref, key_ref, value_ref, cos_ref, sin_ref, sink_ref, late_ref, out_ref):
    filled = len_ref[first_row + pl.program_id(0)]
    lead, _, inner, width = proj_ref.shape
    steps = lead * inner
    pairs = (width // 128) - 1
    slots2 = key_ref.shape[2]
    part = slots2 // parts
    x = proj_ref[...].reshape(steps, width)
    cosines = cos_ref[0]
    sines = sin_ref[0]
    lane = lax.broadcasted_iota(jnp.int32, (steps, 128), 1)
    low = lane < 64
    first = (lane & 63) < 32
    score_scale = HEAD_DIM ** (-0.5) * LOG2E

    def rotated(block):
        swapped = jnp.where(first, pltpu.roll(block, 96, 1), pltpu.roll(block, 32, 1))
        return block * cosines + swapped * sines

    even_rows, odd_rows = [], []
    zero = jnp.zeros((steps, 128), jnp.float32)
    for i in range(pairs):
        turned = rotated(x[:, 128 * i : 128 * i + 128]) * score_scale
        other = pltpu.roll(turned, 64, 1)
        even_rows += [jnp.where(low, turned, zero), jnp.where(low, other, zero)]
        odd_rows += [jnp.where(low, zero, other), jnp.where(low, zero, turned)]
    query_even = jnp.concatenate(even_rows, axis=0).astype(jnp.bfloat16)
    query_odd = jnp.concatenate(odd_rows, axis=0).astype(jnp.bfloat16)
    pair = x[:, 128 * pairs :]
    fresh = jnp.where(low, rotated(pair), pair).astype(jnp.bfloat16)
    rows = query_even.shape[0]
    transposed = (((1,), (1,)), ((), ()))
    new_scores = lax.dot_general(query_even, fresh, transposed, preferred_element_type=jnp.float32)
    new_scores = new_scores + late_ref[...]
    sink = sink_ref[0][:, :1]
    used = (filled + (2 * part - 1)) // (2 * part)
    one = jnp.ones((), jnp.bfloat16)
    fresh_odd = jnp.where(low, one, fresh)

    for count in range(1, parts + 1):

        @pl.when(used == count)
        def _():
            span = count * part
            keys = key_ref[0, 0, :span, :]
            values = value_ref[0, 0, :span, :]
            low_lane = lax.broadcasted_iota(jnp.int32, (span, 128), 1) < 64
            even = lax.dot_general(query_even, keys, transposed, preferred_element_type=jnp.float32)
            odd = lax.dot_general(query_odd, keys, transposed, preferred_element_type=jnp.float32)
            slot = 2 * (lax.broadcasted_iota(jnp.int32, (rows, part), 1) + (span - part))

            def masked(scores, offset):
                last = jnp.where(slot + offset < filled, scores[:, span - part :], masked_score)
                return jnp.concatenate([scores[:, : span - part], last], axis=1) if count > 1 else last

            even = masked(even, 0)
            odd = masked(odd, 1)
            top = jnp.max(jnp.maximum(even, odd), axis=1, keepdims=True)
            top = jnp.maximum(top, jnp.max(new_scores, axis=1, keepdims=True))
            top = jnp.maximum(top, sink)
            even = jnp.exp2(even - top).astype(jnp.bfloat16)
            odd = jnp.exp2(odd - top).astype(jnp.bfloat16)
            new = jnp.exp2(new_scores - top).astype(jnp.bfloat16)
            from_even = jnp.dot(even, jnp.where(low_lane, values, one), preferred_element_type=jnp.float32)
            from_odd = jnp.dot(odd, jnp.where(low_lane, one, values), preferred_element_type=jnp.float32)
            from_odd = from_odd + jnp.dot(new, fresh_odd, preferred_element_type=jnp.float32)
            mixed = from_even + pltpu.roll(from_odd, 64, 1)
            swapped = pltpu.roll(mixed, 64, 1)
            sink_part = jnp.exp2(sink - top)
            for i in range(pairs):
                left = slice(2 * i * steps, (2 * i + 1) * steps)
                right = slice((2 * i + 1) * steps, (2 * i + 2) * steps)
                upper = jnp.where(low, mixed[left], swapped[right])
                total = jnp.where(
                    low, swapped[left] + sink_part[left], mixed[right] + sink_part[right]
                )
                out_ref[:, 0, :, 128 * i : 128 * i + 128] = (
                    (upper / total).reshape(lead, inner, 128).astype(out_ref.dtype)
                )


def attend(first_row, projected, lengths, keys, values, cosines, sines, sinks, late, kv_count):
    lead, row_count, inner, width = projected.shape
    kv_width = width // kv_count
    out_width = kv_width - 2 * HEAD_DIM
    slots2 = keys.shape[2]
    parts = 4 if slots2 % 512 == 0 else 1
    grid_spec = pltpu.PrefetchScalarGridSpec(
        num_scalar_prefetch=1,
        grid=(row_count, kv_count),
        in_specs=[
            pl.BlockSpec((lead, 1, inner, kv_width), lambda b, j, n: (0, b, 0, j)),
            pl.BlockSpec((1, 1, slots2, 128), lambda b, j, n: (j, b + first_row, 0, 0)),
            pl.BlockSpec((1, 1, slots2, 128), lambda b, j, n: (j, b + first_row, 0, 0)),
            pl.BlockSpec((1, lead * inner, 128), lambda b, j, n: (b + first_row, 0, 0)),
            pl.BlockSpec((1, lead * inner, 128), lambda b, j, n: (b + first_row, 0, 0)),
            pl.BlockSpec((1,) + sinks.shape[1:], lambda b, j, n: (j, 0, 0)),
            pl.BlockSpec(late.shape, lambda b, j, n: (0, 0)),
        ],
        out_specs=pl.BlockSpec((lead, 1, inner, out_width), lambda b, j, n: (0, b, 0, j)),
    )
    return pl.pallas_call(
        functools.partial(attend_kernel, first_row, parts),
        grid_spec=grid_spec,
        out_shape=jax.ShapeDtypeStruct((lead, row_count, inner, kv_count * out_width), jnp.bfloat16),
        compiler_params=pltpu.CompilerParams(vmem_limit_bytes=32 * 1024 * 1024),
        cost_estimate=pl.CostEstimate(
            flops=row_count * kv_count * 2 * 2 * 512 * 512 * 128,
            bytes_accessed=row_count * kv_count * slots2 * 512,
            transcendentals=row_count * kv_count * 256 * 1024,
        ),
    )(lengths, projected, keys, values, cosines, sines, sinks, late)


def split(values):
    high = values.astype(jnp.bfloat16)
    return high, (values - high.astype(jnp.float32)).astype(jnp.bfloat16)


def outer_sum(left, right):
    left_high, left_low = split(left)
    right_high, right_low = split(right)
    return lax.dot_general(
        jnp.concatenate([left_high, left_high, left_low], axis=0),
        jnp.concatenate([right_high, right_low, right_high], axis=0),
        (((0,), (0,)), ((), ())),
        preferred_element_type=jnp.float32,
    )


def crossed(block, axis, mask):
    count = lax.axis_size(axis)
    return lax.ppermute(block, axis, [(i, i ^ mask) for i in range(count)])


def first_blocks(own, heads):
    blocks = {m: crossed(own, "head", m) for m in range(1, heads) if m == 1 or m % 2 == 0}
    return {0: own, **blocks}


def first_hop(partial, heads):
    passed = []
    for m in range(2, heads, 2):
        extra = crossed(partial[m + 1], "head", 1).astype(jnp.float32)
        passed.append((partial[m].astype(jnp.float32) + extra).astype(jnp.bfloat16))
    return partial[0], partial[1], passed


def second_hop(own, near, passed):
    received = [crossed(block, "head", 2 * i + 2) for i, block in enumerate(passed)]
    return own, [crossed(near, "head", 1)] + received


def total_of(own, received):
    return sum([block.astype(jnp.float32) for block in received], own.astype(jnp.float32)).astype(
        jnp.bfloat16
    )


def shards(
    hidden,
    joined_weight,
    output_weight,
    key_cache,
    value_cache,
    sink_logits,
    lengths,
    query_left,
    query_right,
    output_left,
    output_right,
    fitness,
    query_master,
    query_moment,
    output_master,
    output_moment,
):
    model, kv_count, kv_width = joined_weight.shape
    group = kv_width // HEAD_DIM - 2
    q_width = group * HEAD_DIM
    heads = lax.axis_size("head")
    members = lax.axis_size("member")
    _, own_steps, row_count, _ = hidden.shape
    steps = heads * own_steps
    feature_count = heads * output_weight.shape[0]
    query_scale = noise_scale / math.sqrt(model)
    output_scale = noise_scale / math.sqrt(feature_count)
    bounds = [0]
    for share in SHARES:
        bounds.append(bounds[-1] + row_count // share)

    local = hidden[0].transpose(1, 0, 2)
    first_landed = first_blocks(local[: bounds[1]], heads)

    def gather_rest(landed):
        gathered = []
        for first_row, end_row in zip(bounds[1:], bounds[2:] + [None]):
            blocks = dict(landed)
            for m in range(3, heads, 2):
                blocks[m] = crossed(blocks[m - 1], "head", 1)
            gathered.append(jnp.stack([blocks[m] for m in range(heads)]))
            if end_row is not None:
                own, _ = lax.optimization_barrier((local[first_row:end_row], landed))
                landed = first_blocks(own, heads)
        return gathered

    factors = jnp.concatenate(
        [query_left, output_right, query_right * fitness[0], output_left * fitness[0]], axis=2
    ).astype(jnp.bfloat16)
    every, distance = factors[0], 1
    if members & (members - 1):
        every = lax.all_gather(every, "member", axis=0, tiled=True)
        distance = members

    right_padded = jnp.pad(
        (query_right[0] * query_scale).reshape(-1, kv_count, q_width),
        ((0, 0), (0, 0), (0, kv_width - q_width)),
    ).reshape(-1, kv_count * kv_width)
    flat_weight = joined_weight.reshape(model, kv_count * kv_width)
    out_factor = output_right[0] * output_scale
    pair_count = key_cache.shape[-1] // 128
    keys = key_cache[0].reshape(kv_count, row_count, pair_count, 128)
    values = value_cache[0].reshape(kv_count, row_count, pair_count, 128)
    flat_weight, keys, values, out_factor, first_landed = lax.optimization_barrier(
        (flat_weight, keys, values, out_factor, first_landed)
    )
    gathered = gather_rest(first_landed)
    in_weight = (flat_weight.astype(jnp.float32) + outer_sum(query_left[0], right_padded)).astype(
        jnp.bfloat16
    )
    out_weight = (
        output_weight.T.astype(jnp.float32)
        + outer_sum(out_factor, output_left[0])
    ).astype(jnp.bfloat16)

    half_dim = HEAD_DIM // 2
    exponents = jnp.arange(half_dim, dtype=jnp.float32) * (-2.0 / HEAD_DIM)
    frequency = jnp.power(jnp.float32(rotary_base), exponents)
    owners = lax.axis_index("head") ^ jnp.arange(heads, dtype=jnp.int32)
    step_ids = (owners[:, None] * own_steps + jnp.arange(own_steps, dtype=jnp.int32)).reshape(-1)
    positions = lengths[0][:, None] + step_ids[None, :]
    angles = positions.astype(jnp.float32)[..., None] * frequency
    cosines = jnp.cos(angles)
    sines = jnp.sin(angles)
    cosines = jnp.concatenate([cosines, cosines, cosines, cosines], axis=-1)
    sines = jnp.concatenate([-sines, sines, -sines, sines], axis=-1)
    late = jnp.where(step_ids[None, :] <= step_ids[:, None], 0.0, masked_score)
    late = jnp.broadcast_to(late[None], (group, steps, steps)).reshape(group * steps, steps)
    late = late.astype(jnp.float32)
    sinks = jnp.broadcast_to(
        (sink_logits * LOG2E).reshape(kv_count, group, 1, 1), (kv_count, group, steps, 128)
    ).reshape(kv_count, group * steps, 128)

    pieces = []
    partial, hopped = None, None
    for c, (first_row, end_row) in enumerate(zip(bounds[:-1], bounds[1:])):
        chunk = end_row - first_row
        token_rows = gathered[c].reshape(-1, model)
        if partial is not None:
            token_rows, partial = lax.optimization_barrier((token_rows, partial))
        projected = jnp.dot(token_rows, in_weight, preferred_element_type=jnp.float32)
        projected = projected.reshape(heads, chunk, own_steps, kv_count * kv_width)
        if own_steps % 8:
            projected = projected.transpose(1, 0, 2, 3).reshape(1, chunk, steps, kv_count * kv_width)
        attended = attend(
            first_row, projected, lengths[0], keys, values, cosines, sines, sinks, late, kv_count
        )
        landed = None if hopped is None else second_hop(*hopped)
        hopped = None if partial is None else first_hop(partial, heads)
        if distance < members:
            every = jnp.concatenate([every, crossed(every, "member", distance)], axis=0)
            distance *= 2
        attended, landed, hopped, every = lax.optimization_barrier((attended, landed, hopped, every))
        if landed is not None:
            pieces.append(total_of(*landed).reshape(-1, own_steps, model))
        flat = attended
        if own_steps % 8:
            flat = attended.reshape(chunk, heads, own_steps, -1).transpose(1, 0, 2, 3)
        flat = flat.reshape(heads * chunk * own_steps, -1)
        partial = lax.dot_general(
            flat, out_weight, (((1,), (1,)), ((), ())), preferred_element_type=jnp.float32
        ).astype(jnp.bfloat16)
        partial = partial.reshape(heads, chunk * own_steps, model)
    landed = second_hop(*hopped)
    pieces.append(total_of(*landed).reshape(-1, own_steps, model))
    landed = second_hop(*first_hop(partial, heads))
    pieces.append(total_of(*landed).reshape(-1, own_steps, model))
    layer_output = jnp.concatenate(pieces, axis=0).transpose(1, 0, 2)[None]

    while distance < members:
        every = jnp.concatenate([every, crossed(every, "member", distance)], axis=0)
        distance *= 2
    row_share, columns = query_master.shape
    row_start = lax.axis_index("member") * row_share
    left_query = lax.dynamic_slice_in_dim(every, row_start, row_share, 1)
    left_output = lax.dynamic_slice_in_dim(every, model + row_start, row_share, 1)
    right_query = every[:, 2 * model : 2 * model + columns]
    right_output = every[:, 2 * model + columns :]

    def stepped(left, right):
        total = lax.dot_general(
            left, right, (((0,), (0,)), ((), ())), preferred_element_type=jnp.float32
        )
        return total / members

    query_momenta = moment_decay * query_moment + stepped(left_query, right_query)
    output_momenta = moment_decay * output_moment + stepped(left_output, right_output)
    query_weights = query_master + learn_rate * query_momenta
    output_weights = output_master + learn_rate * output_momenta
    return (layer_output, query_weights, query_momenta, output_weights, output_momenta)


def layer_kernel(
    heads,
    members,
    bounds,
    kv_count,
    scales,
    length_ref,
    sink_ref,
    own_ref,
    weight_hbm,
    key_hbm,
    value_hbm,
    out_weight_hbm,
    left_ref,
    right_ref,
    out_left_ref,
    out_right_ref,
    frequency_ref,
    factor_ref,
    out_ref,
    every_ref,
    weight_ref,
    key_ref,
    value_ref,
    out_weight_ref,
    cos_ref,
    sin_ref,
    late_ref,
    gathered,
    partial,
    from_left,
    from_right,
    projected,
    attended,
    load_sem,
    gather_sem,
    right_sem,
    left_sem,
    sum_right_sem,
    sum_left_sem,
    right_sum_sem,
    left_sum_sem,
    factor_send,
    factor_recv,
):
    me = lax.axis_index("head")
    mine = lax.axis_index("member")
    last = heads - 1
    chunks = len(bounds) - 1
    row_count = bounds[-1]
    inner = own_ref.shape[0] // row_count
    width = projected.shape[2] // kv_count
    pairs = width // 128 - 1
    out_width = pairs * 128
    steps = heads * inner
    right = {"head": jnp.minimum(me + 1, last)}
    left = {"head": jnp.maximum(me - 1, 0)}
    mesh_id = pl.DeviceIdType.MESH

    loads = [
        pltpu.make_async_copy(source, target, load_sem.at[i])
        for i, (source, target) in enumerate(
            [
                (own_ref, gathered.at[me]),
                (weight_hbm, weight_ref),
                (key_hbm, key_ref),
                (value_hbm, value_ref),
                (out_weight_hbm, out_weight_ref),
            ]
        )
    ]
    barrier = pltpu.get_barrier_semaphore()

    @pl.when(me > 0)
    def _():
        pl.semaphore_signal(barrier, inc=1, device_id=left, device_id_type=mesh_id)

    @pl.when(me < last)
    def _():
        pl.semaphore_signal(barrier, inc=1, device_id=right, device_id_type=mesh_id)

    def peer(o):
        return {"member": lax.rem(mine + o, members)}

    for o in range(1, members):
        pl.semaphore_signal(barrier, inc=1, device_id=peer(o), device_id_type=mesh_id)
    neighbours = jnp.where(me > 0, 1, 0) + jnp.where(me < last, 1, 0) + (members - 1)
    pl.semaphore_wait(barrier, neighbours)

    def push(source, target, send, receive, device):
        return pltpu.make_async_remote_copy(
            src_ref=source,
            dst_ref=target,
            send_sem=send,
            recv_sem=receive,
            device_id=device,
            device_id_type=mesh_id,
        )

    def span(c):
        return pl.ds(bounds[c] * inner, (bounds[c + 1] - bounds[c]) * inner)

    def own_copy(c, send, device):
        return push(
            own_ref.at[span(c)], gathered.at[me, span(c)], send.at[me, c], gather_sem.at[me, c], device
        )

    def block_copy(k, c, send, device):
        block = gathered.at[k, span(c)]
        return push(block, block, send.at[k, c], gather_sem.at[k, c], device)

    def send_own(c):
        @pl.when(me < last)
        def _():
            own_copy(c, right_sem, right).start()

        @pl.when(me > 0)
        def _():
            own_copy(c, left_sem, left).start()

    def forward(t, c):
        k = jnp.maximum(me - t, 0)

        @pl.when((me >= t) & (me < last))
        def _():
            block_copy(k, c, right_sem, right).wait_recv()
            block_copy(k, c, right_sem, right).start()

        n = jnp.minimum(me + t, last)

        @pl.when((me + t <= last) & (me > 0))
        def _():
            block_copy(n, c, left_sem, left).wait_recv()
            block_copy(n, c, left_sem, left).start()

    def land(c):
        for t in range(1, heads):

            @pl.when((me == last) & (me >= t))
            def _():
                block_copy(jnp.maximum(me - t, 0), c, right_sem, right).wait_recv()

            @pl.when((me == 0) & (me + t <= last))
            def _():
                block_copy(jnp.minimum(me + t, last), c, left_sem, left).wait_recv()

    def right_sum(d, c):
        return push(
            partial.at[d, span(c)],
            from_left.at[d, span(c)],
            sum_right_sem.at[d, c],
            right_sum_sem.at[d, c],
            right,
        )

    def left_sum(d, c):
        return push(
            partial.at[d, span(c)],
            from_right.at[d, span(c)],
            sum_left_sem.at[d, c],
            left_sum_sem.at[d, c],
            left,
        )

    def add_in(d, c, landed):
        total = partial[d, span(c)].astype(jnp.float32) + landed[d, span(c)].astype(jnp.float32)
        partial[d, span(c)] = total.astype(partial.dtype)

    def sum_first(c):
        @pl.when(me == 0)
        def _():
            for d in range(last, 0, -1):
                right_sum(d, c).start()

        @pl.when(me == last)
        def _():
            for d in range(last):
                left_sum(d, c).start()

    def right_next(c):
        for d in range(last, 1, -1):

            @pl.when((me > 0) & (me < d))
            def _():
                right_sum(d, c).wait_recv()
                add_in(d, c, from_left)
                right_sum(d, c).start()

    def left_next(c):
        for d in range(last - 1):

            @pl.when((me < last) & (me > d))
            def _():
                left_sum(d, c).wait_recv()
                add_in(d, c, from_right)
                left_sum(d, c).start()

    def sum_next(c):
        @pl.when(2 * me < last)
        def _():
            right_next(c)
            left_next(c)

        @pl.when(2 * me >= last)
        def _():
            left_next(c)
            right_next(c)

    def sum_last(c):
        total = partial[me, span(c)].astype(jnp.float32)

        @pl.when(me > 0)
        def _():
            right_sum(me, c).wait_recv()

        @pl.when(me < last)
        def _():
            left_sum(me, c).wait_recv()

        @pl.when((me > 0) & (me < last))
        def _():
            both = from_left[me, span(c)].astype(jnp.float32)
            both = both + from_right[me, span(c)].astype(jnp.float32)
            out_ref[span(c)] = (total + both).astype(out_ref.dtype)

        @pl.when(me == 0)
        def _():
            out_ref[span(c)] = (total + from_right[me, span(c)].astype(jnp.float32)).astype(out_ref.dtype)

        @pl.when(me == last)
        def _():
            out_ref[span(c)] = (total + from_left[me, span(c)].astype(jnp.float32)).astype(out_ref.dtype)

    def factor_copy(o):
        return push(factor_ref, every_ref.at[mine], factor_send.at[o], factor_recv.at[o], peer(o))

    send_own(0)
    if chunks > 1:
        send_own(1)
    for o in range(1, members):
        factor_copy(o).start()
    for load in loads:
        load.start()
    every_ref[mine] = factor_ref[...]

    lane = lax.broadcasted_iota(jnp.int32, (steps, 128), 1)
    low = lane < HEAD_DIM
    first = (lane & (HEAD_DIM - 1)) < HEAD_DIM // 2
    score_scale = HEAD_DIM ** (-0.5) * LOG2E
    transposed = (((1,), (1,)), ((), ()))
    one = jnp.ones((), jnp.bfloat16)
    group = 2 * pairs
    pair_count = key_ref.shape[2]
    slot = 2 * lax.broadcasted_iota(jnp.int32, (8, pair_count), 1)
    in_scale, out_scale = scales

    def tables(b, carry):
        step = lax.broadcasted_iota(jnp.int32, (steps, 128), 0)
        angles = (step + length_ref[b]).astype(jnp.float32) * frequency_ref[...]
        cos_ref[b] = jnp.cos(angles)
        sines = jnp.sin(angles)
        sin_ref[b] = jnp.where(first, -sines, sines)
        return carry

    lax.fori_loop(0, row_count, tables, 0)
    query_step = lax.broadcasted_iota(jnp.int32, (steps, steps), 0)
    new_step = lax.broadcasted_iota(jnp.int32, (steps, steps), 1)
    late = jnp.where(new_step <= query_step, 0.0, masked_score).astype(jnp.float32)
    for i in range(group):
        late_ref[i * steps : (i + 1) * steps] = late
    in_left = left_ref[...].astype(jnp.bfloat16)
    out_left = out_left_ref[...].astype(jnp.bfloat16)

    def project(c):
        size = (bounds[c + 1] - bounds[c]) * inner
        x = gathered[:, span(c), :].reshape(heads * size, -1)
        thin = lax.dot_general(x, in_left, transposed, preferred_element_type=jnp.float32)
        thin = thin.astype(jnp.bfloat16)
        for j in range(kv_count):
            columns = slice(j * width, (j + 1) * width)
            tile = jnp.dot(x, weight_ref[:, columns], preferred_element_type=jnp.float32)
            factor = right_ref[:, j * out_width : (j + 1) * out_width] * in_scale
            high, rest = split(factor)
            extra = jnp.dot(thin, high, preferred_element_type=jnp.float32)
            extra = extra + jnp.dot(thin, rest, preferred_element_type=jnp.float32)
            query = tile[:, :out_width] + extra
            start = j * width
            projected[:, :size, start : start + out_width] = query.reshape(heads, size, -1)
            projected[:, :size, start + out_width : start + width] = tile[:, out_width:].reshape(
                heads, size, -1
            )

    def attend_one(b, s, j):
        place = pl.ds(pl.multiple_of(s * inner, inner), inner)
        x = projected[:, place, j * width : (j + 1) * width].reshape(steps, width)
        cosines = cos_ref[b]
        sines = sin_ref[b]

        def rotated(block):
            swapped = jnp.where(first, pltpu.roll(block, 96, 1), pltpu.roll(block, 32, 1))
            return block * cosines + swapped * sines

        even_rows, odd_rows = [], []
        zero = jnp.zeros((steps, 128), jnp.float32)
        for i in range(pairs):
            turned = rotated(x[:, 128 * i : 128 * i + 128]) * score_scale
            other = pltpu.roll(turned, 64, 1)
            even_rows += [jnp.where(low, turned, zero), jnp.where(low, other, zero)]
            odd_rows += [jnp.where(low, zero, other), jnp.where(low, zero, turned)]
        query_even = jnp.concatenate(even_rows, axis=0).astype(jnp.bfloat16)
        query_odd = jnp.concatenate(odd_rows, axis=0).astype(jnp.bfloat16)
        pair = x[:, 128 * pairs :]
        fresh = jnp.where(low, rotated(pair), pair).astype(jnp.bfloat16)
        new_scores = lax.dot_general(query_even, fresh, transposed, preferred_element_type=jnp.float32)
        new_scores = new_scores + late_ref[...]
        sink = jnp.concatenate(
            [jnp.full((steps, 1), sink_ref[j * group + i] * LOG2E) for i in range(group)], axis=0
        )
        fresh_odd = jnp.where(low, one, fresh)
        keys = key_ref[j, b]
        values = value_ref[j, b]
        filled = length_ref[b]
        even_bias = jnp.where(slot < filled, 0.0, masked_score)[0:1]
        odd_bias = jnp.where(slot + 1 < filled, 0.0, masked_score)[0:1]
        low_lane = lax.broadcasted_iota(jnp.int32, values.shape, 1) < HEAD_DIM
        even = lax.dot_general(query_even, keys, transposed, preferred_element_type=jnp.float32)
        odd = lax.dot_general(query_odd, keys, transposed, preferred_element_type=jnp.float32)
        even = even + even_bias
        odd = odd + odd_bias
        top = jnp.max(jnp.maximum(even, odd), axis=1, keepdims=True)
        top = jnp.maximum(top, jnp.max(new_scores, axis=1, keepdims=True))
        top = jnp.maximum(top, sink)
        even = jnp.exp2(even - top).astype(jnp.bfloat16)
        odd = jnp.exp2(odd - top).astype(jnp.bfloat16)
        new = jnp.exp2(new_scores - top).astype(jnp.bfloat16)
        from_even = jnp.dot(even, jnp.where(low_lane, values, one), preferred_element_type=jnp.float32)
        from_odd = jnp.dot(odd, jnp.where(low_lane, one, values), preferred_element_type=jnp.float32)
        from_odd = from_odd + jnp.dot(new, fresh_odd, preferred_element_type=jnp.float32)
        mixed = from_even + pltpu.roll(from_odd, 64, 1)
        swapped = pltpu.roll(mixed, 64, 1)
        sink_part = jnp.exp2(sink - top)
        for i in range(pairs):
            near = slice(2 * i * steps, (2 * i + 1) * steps)
            far = slice((2 * i + 1) * steps, (2 * i + 2) * steps)
            upper = jnp.where(low, mixed[near], swapped[far])
            total = jnp.where(low, swapped[near] + sink_part[near], mixed[far] + sink_part[far])
            start = j * out_width + 128 * i
            attended[:, place, start : start + 128] = (upper / total).reshape(heads, inner, 128)

    def put_out(c):
        size = (bounds[c + 1] - bounds[c]) * inner
        x = attended[:, :size].reshape(heads * size, -1).astype(jnp.bfloat16)
        thin = lax.dot_general(x, out_left, transposed, preferred_element_type=jnp.float32)
        thin = thin.astype(jnp.bfloat16)
        model = out_weight_ref.shape[0]
        for start in range(0, model, 768):
            columns = slice(start, min(start + 768, model))
            tile = lax.dot_general(
                x, out_weight_ref[columns], transposed, preferred_element_type=jnp.float32
            )
            high, rest = split(out_right_ref[:, columns] * out_scale)
            tile = tile + jnp.dot(thin, high, preferred_element_type=jnp.float32)
            tile = tile + jnp.dot(thin, rest, preferred_element_type=jnp.float32)
            partial[:, span(c), columns] = tile.astype(partial.dtype).reshape(heads, size, -1)

    for c in range(chunks):
        if c == 0:
            for t in range(1, heads):
                forward(t, c)
            for n in range(2, chunks):
                send_own(n)
            loads[0].wait()
        land(c)
        if c == 0:
            loads[1].wait()
        project(c)
        if c == 0:
            loads[2].wait()
            loads[3].wait()
        count = bounds[c + 1] - bounds[c]

        def attend_rows(s, carry):
            for j in range(kv_count):
                attend_one(bounds[c] + s, s, j)
            if c + 1 < chunks:
                for t in range(1, heads - 1):

                    @pl.when(s == max(count - heads + 1 + t, 0))
                    def _():
                        forward(t, c + 1)

            return carry

        lax.fori_loop(0, count, attend_rows, 0)
        if c == 0:
            loads[4].wait()
        put_out(c)
        sum_first(c)
        if c > 0:
            sum_next(c - 1)
    for c in range(chunks - 2):
        sum_last(c)
    sum_next(chunks - 1)
    for o in range(1, members):
        factor_copy(o).wait_recv()
    for c in range(max(chunks - 2, 0), chunks):
        sum_last(c)

    for o in range(1, members):
        factor_copy(o).wait_send()
    for c in range(chunks):

        @pl.when(me < last)
        def _():
            own_copy(c, right_sem, right).wait_send()

        @pl.when(me > 0)
        def _():
            own_copy(c, left_sem, left).wait_send()

        for k in range(heads):

            @pl.when((k < me) & (me < last))
            def _():
                block_copy(k, c, right_sem, right).wait_send()

            @pl.when((k > me) & (me > 0))
            def _():
                block_copy(k, c, left_sem, left).wait_send()

            @pl.when(k > me)
            def _():
                right_sum(k, c).wait_send()

            @pl.when(k < me)
            def _():
                left_sum(k, c).wait_send()


def whole_layer(operands, heads, members, bounds, kv_count, scales):
    own, weight, keys, out_weight = operands[2], operands[3], operands[4], operands[6]
    row_count = bounds[-1]
    tokens, model = own.shape
    features = out_weight.shape[1]
    inner = tokens // row_count
    steps = heads * inner
    chunks = len(bounds) - 1
    rows = inner * max(b - a for a, b in zip(bounds, bounds[1:]))
    group = features // (kv_count * HEAD_DIM)
    factor = operands[-1]
    vmem = pl.BlockSpec(memory_space=pltpu.VMEM)
    smem = pl.BlockSpec(memory_space=pltpu.SMEM)
    anywhere = pl.BlockSpec(memory_space=pl.ANY)
    dma = pltpu.SemaphoreType.DMA
    block = pltpu.VMEM((heads, tokens, model), jnp.bfloat16)
    return pl.pallas_call(
        functools.partial(layer_kernel, heads, members, bounds, kv_count, scales),
        in_specs=[smem, smem, vmem] + [anywhere] * 4 + [vmem] * 6,
        out_specs=[vmem, vmem],
        out_shape=[
            jax.ShapeDtypeStruct((tokens, model), jnp.bfloat16),
            jax.ShapeDtypeStruct((members,) + factor.shape, jnp.bfloat16),
        ],
        scratch_shapes=[
            pltpu.VMEM(weight.shape, jnp.bfloat16),
            pltpu.VMEM(keys.shape, jnp.bfloat16),
            pltpu.VMEM(keys.shape, jnp.bfloat16),
            pltpu.VMEM(out_weight.shape, jnp.bfloat16),
            pltpu.VMEM((row_count, steps, 128), jnp.float32),
            pltpu.VMEM((row_count, steps, 128), jnp.float32),
            pltpu.VMEM((group * steps, steps), jnp.float32),
            block,
            block,
            block,
            block,
            pltpu.VMEM((heads, rows, weight.shape[1]), jnp.float32),
            pltpu.VMEM((heads, rows, features), jnp.float32),
            dma((5,)),
        ]
        + [dma((heads, chunks))] * 7
        + [dma((members,))] * 2,
        compiler_params=pltpu.CompilerParams(
            collective_id=0, has_side_effects=True, vmem_limit_bytes=VMEM_LIMIT
        ),
    )(*operands)


def fused_shards(
    hidden,
    joined_weight,
    output_weight,
    key_cache,
    value_cache,
    sink_logits,
    lengths,
    query_left,
    query_right,
    output_left,
    output_right,
    fitness,
    query_master,
    query_moment,
    output_master,
    output_moment,
):
    model, kv_count, kv_width = joined_weight.shape
    group = kv_width // HEAD_DIM - 2
    q_width = group * HEAD_DIM
    heads = lax.axis_size("head")
    members = lax.axis_size("member")
    _, own_steps, row_count, _ = hidden.shape
    steps = heads * own_steps
    feature_count = heads * output_weight.shape[0]
    query_scale = noise_scale / math.sqrt(model)
    output_scale = noise_scale / math.sqrt(feature_count)
    own = hidden[0].transpose(1, 0, 2).reshape(row_count * own_steps, model)
    factors = jnp.concatenate(
        [query_left, output_right, query_right * fitness[0], output_left * fitness[0]], axis=2
    ).astype(jnp.bfloat16)
    flat_weight = joined_weight.reshape(model, kv_count * kv_width)
    pair_count = key_cache.shape[-1] // 128
    keys = key_cache[0].reshape(kv_count, row_count, pair_count, 128)
    values = value_cache[0].reshape(kv_count, row_count, pair_count, 128)
    half_dim = HEAD_DIM // 2
    exponents = (jnp.arange(128, dtype=jnp.int32) % half_dim).astype(jnp.float32) * (-2.0 / HEAD_DIM)
    frequency = jnp.power(jnp.float32(rotary_base), exponents)[None]
    bounds = [0]
    for share in SIZES:
        bounds.append(bounds[-1] + row_count * share // sum(SIZES))
    if any((b - a) * own_steps % 16 or a == b for a, b in zip(bounds, bounds[1:])):
        bounds = [0, row_count]
    operands = [
        lengths[0], sink_logits, own, flat_weight, keys, values, output_weight.T,
        query_left[0], query_right[0], output_left[0], output_right[0], frequency, factors[0],
    ]
    layer_rows, every = whole_layer(
        operands, heads, members, bounds, kv_count, (query_scale, output_scale)
    )
    layer_output = layer_rows.reshape(row_count, own_steps, model).transpose(1, 0, 2)[None]
    every = every.reshape(-1, every.shape[-1])

    row_share, columns = query_master.shape
    row_start = lax.axis_index("member") * row_share
    left_query = lax.dynamic_slice_in_dim(every, row_start, row_share, 1)
    left_output = lax.dynamic_slice_in_dim(every, model + row_start, row_share, 1)
    right_query = every[:, 2 * model : 2 * model + columns]
    right_output = every[:, 2 * model + columns :]

    def stepped(left, right):
        total = lax.dot_general(
            left, right, (((0,), (0,)), ((), ())), preferred_element_type=jnp.float32
        )
        return total / members

    query_momenta = moment_decay * query_moment + stepped(left_query, right_query)
    output_momenta = moment_decay * output_moment + stepped(left_output, right_output)
    query_weights = query_master + learn_rate * query_momenta
    output_weights = output_master + learn_rate * output_momenta
    return (layer_output, query_weights, query_momenta, output_weights, output_momenta)


def layer(hidden, *others):
    body = fused_shards if hidden.shape[1] % 8 == 0 else shards
    return body(hidden, *others)


def solution(mesh):
    placed = (
        P("member", "head", None, None),
        P(None, "head", None),
        P("head", None),
        P("member", "head", None, None),
        P("member", "head", None, None),
        P("head"),
        P("member", None),
        P("member", None, None),
        P("member", None, "head"),
        P("member", None, "head"),
        P("member", None, None),
        P("member"),
        P("member", "head"),
        P("member", "head"),
        P("member", "head"),
        P("member", "head"),
    )
    return jax.shard_map(
        layer,
        mesh=mesh,
        in_specs=placed,
        out_specs=(
            P("member", "head", None, None),
            P("member", "head"),
            P("member", "head"),
            P("member", "head"),
            P("member", "head"),
        ),
        check_vma=False,
    )
```

```python
import functools
import math

import jax
import jax.numpy as jnp
from jax import lax
from jax.experimental import pallas as pl
from jax.experimental.pallas import tpu as pltpu
from jax.sharding import PartitionSpec as P

HEAD_DIM = 64
SHARES = (2, 4, 4)
SIZES = (2, 4, 4, 4, 2)
AHEAD = 3
VMEM_LIMIT = 48 * 1024 * 1024

rotary_base = 150000.0
noise_scale = 0.5
moment_decay = 0.9
learn_rate = 0.2
masked_score = -1e30
LOG2E = 1.4426950408889634


def attend_kernel(first_row, parts, len_ref, proj_ref, key_ref, value_ref, cos_ref, sin_ref, sink_ref, late_ref, out_ref):
    filled = len_ref[first_row + pl.program_id(0)]
    lead, _, inner, width = proj_ref.shape
    steps = lead * inner
    pairs = (width // 128) - 1
    slots2 = key_ref.shape[2]
    part = slots2 // parts
    x = proj_ref[...].reshape(steps, width)
    cosines = cos_ref[0]
    sines = sin_ref[0]
    lane = lax.broadcasted_iota(jnp.int32, (steps, 128), 1)
    low = lane < 64
    first = (lane & 63) < 32
    score_scale = HEAD_DIM ** (-0.5) * LOG2E

    def rotated(block):
        swapped = jnp.where(first, pltpu.roll(block, 96, 1), pltpu.roll(block, 32, 1))
        return block * cosines + swapped * sines

    even_rows, odd_rows = [], []
    zero = jnp.zeros((steps, 128), jnp.float32)
    for i in range(pairs):
        turned = rotated(x[:, 128 * i : 128 * i + 128]) * score_scale
        other = pltpu.roll(turned, 64, 1)
        even_rows += [jnp.where(low, turned, zero), jnp.where(low, other, zero)]
        odd_rows += [jnp.where(low, zero, other), jnp.where(low, zero, turned)]
    query_even = jnp.concatenate(even_rows, axis=0).astype(jnp.bfloat16)
    query_odd = jnp.concatenate(odd_rows, axis=0).astype(jnp.bfloat16)
    pair = x[:, 128 * pairs :]
    fresh = jnp.where(low, rotated(pair), pair).astype(jnp.bfloat16)
    rows = query_even.shape[0]
    transposed = (((1,), (1,)), ((), ()))
    new_scores = lax.dot_general(query_even, fresh, transposed, preferred_element_type=jnp.float32)
    new_scores = new_scores + late_ref[...]
    sink = sink_ref[0][:, :1]
    used = (filled + (2 * part - 1)) // (2 * part)
    one = jnp.ones((), jnp.bfloat16)
    fresh_odd = jnp.where(low, one, fresh)

    for count in range(1, parts + 1):

        @pl.when(used == count)
        def _():
            span = count * part
            keys = key_ref[0, 0, :span, :]
            values = value_ref[0, 0, :span, :]
            low_lane = lax.broadcasted_iota(jnp.int32, (span, 128), 1) < 64
            even = lax.dot_general(query_even, keys, transposed, preferred_element_type=jnp.float32)
            odd = lax.dot_general(query_odd, keys, transposed, preferred_element_type=jnp.float32)
            slot = 2 * (lax.broadcasted_iota(jnp.int32, (rows, part), 1) + (span - part))

            def masked(scores, offset):
                last = jnp.where(slot + offset < filled, scores[:, span - part :], masked_score)
                return jnp.concatenate([scores[:, : span - part], last], axis=1) if count > 1 else last

            even = masked(even, 0)
            odd = masked(odd, 1)
            top = jnp.max(jnp.maximum(even, odd), axis=1, keepdims=True)
            top = jnp.maximum(top, jnp.max(new_scores, axis=1, keepdims=True))
            top = jnp.maximum(top, sink)
            even = jnp.exp2(even - top).astype(jnp.bfloat16)
            odd = jnp.exp2(odd - top).astype(jnp.bfloat16)
            new = jnp.exp2(new_scores - top).astype(jnp.bfloat16)
            from_even = jnp.dot(even, jnp.where(low_lane, values, one), preferred_element_type=jnp.float32)
            from_odd = jnp.dot(odd, jnp.where(low_lane, one, values), preferred_element_type=jnp.float32)
            from_odd = from_odd + jnp.dot(new, fresh_odd, preferred_element_type=jnp.float32)
            mixed = from_even + pltpu.roll(from_odd, 64, 1)
            swapped = pltpu.roll(mixed, 64, 1)
            sink_part = jnp.exp2(sink - top)
            for i in range(pairs):
                left = slice(2 * i * steps, (2 * i + 1) * steps)
                right = slice((2 * i + 1) * steps, (2 * i + 2) * steps)
                upper = jnp.where(low, mixed[left], swapped[right])
                total = jnp.where(
                    low, swapped[left] + sink_part[left], mixed[right] + sink_part[right]
                )
                out_ref[:, 0, :, 128 * i : 128 * i + 128] = (
                    (upper / total).reshape(lead, inner, 128).astype(out_ref.dtype)
                )


def attend(first_row, projected, lengths, keys, values, cosines, sines, sinks, late, kv_count):
    lead, row_count, inner, width = projected.shape
    kv_width = width // kv_count
    out_width = kv_width - 2 * HEAD_DIM
    slots2 = keys.shape[2]
    parts = 4 if slots2 % 512 == 0 else 1
    grid_spec = pltpu.PrefetchScalarGridSpec(
        num_scalar_prefetch=1,
        grid=(row_count, kv_count),
        in_specs=[
            pl.BlockSpec((lead, 1, inner, kv_width), lambda b, j, n: (0, b, 0, j)),
            pl.BlockSpec((1, 1, slots2, 128), lambda b, j, n: (j, b + first_row, 0, 0)),
            pl.BlockSpec((1, 1, slots2, 128), lambda b, j, n: (j, b + first_row, 0, 0)),
            pl.BlockSpec((1, lead * inner, 128), lambda b, j, n: (b + first_row, 0, 0)),
            pl.BlockSpec((1, lead * inner, 128), lambda b, j, n: (b + first_row, 0, 0)),
            pl.BlockSpec((1,) + sinks.shape[1:], lambda b, j, n: (j, 0, 0)),
            pl.BlockSpec(late.shape, lambda b, j, n: (0, 0)),
        ],
        out_specs=pl.BlockSpec((lead, 1, inner, out_width), lambda b, j, n: (0, b, 0, j)),
    )
    return pl.pallas_call(
        functools.partial(attend_kernel, first_row, parts),
        grid_spec=grid_spec,
        out_shape=jax.ShapeDtypeStruct((lead, row_count, inner, kv_count * out_width), jnp.bfloat16),
        compiler_params=pltpu.CompilerParams(vmem_limit_bytes=32 * 1024 * 1024),
        cost_estimate=pl.CostEstimate(
            flops=row_count * kv_count * 2 * 2 * 512 * 512 * 128,
            bytes_accessed=row_count * kv_count * slots2 * 512,
            transcendentals=row_count * kv_count * 256 * 1024,
        ),
    )(lengths, projected, keys, values, cosines, sines, sinks, late)


def split(values):
    high = values.astype(jnp.bfloat16)
    return high, (values - high.astype(jnp.float32)).astype(jnp.bfloat16)


def outer_sum(left, right):
    left_high, left_low = split(left)
    right_high, right_low = split(right)
    return lax.dot_general(
        jnp.concatenate([left_high, left_high, left_low], axis=0),
        jnp.concatenate([right_high, right_low, right_high], axis=0),
        (((0,), (0,)), ((), ())),
        preferred_element_type=jnp.float32,
    )


def crossed(block, axis, mask):
    count = lax.axis_size(axis)
    return lax.ppermute(block, axis, [(i, i ^ mask) for i in range(count)])


def first_blocks(own, heads):
    blocks = {m: crossed(own, "head", m) for m in range(1, heads) if m == 1 or m % 2 == 0}
    return {0: own, **blocks}


def first_hop(partial, heads):
    passed = []
    for m in range(2, heads, 2):
        extra = crossed(partial[m + 1], "head", 1).astype(jnp.float32)
        passed.append((partial[m].astype(jnp.float32) + extra).astype(jnp.bfloat16))
    return partial[0], partial[1], passed


def second_hop(own, near, passed):
    received = [crossed(block, "head", 2 * i + 2) for i, block in enumerate(passed)]
    return own, [crossed(near, "head", 1)] + received


def total_of(own, received):
    return sum([block.astype(jnp.float32) for block in received], own.astype(jnp.float32)).astype(
        jnp.bfloat16
    )


def shards(
    hidden,
    joined_weight,
    output_weight,
    key_cache,
    value_cache,
    sink_logits,
    lengths,
    query_left,
    query_right,
    output_left,
    output_right,
    fitness,
    query_master,
    query_moment,
    output_master,
    output_moment,
):
    model, kv_count, kv_width = joined_weight.shape
    group = kv_width // HEAD_DIM - 2
    q_width = group * HEAD_DIM
    heads = lax.axis_size("head")
    members = lax.axis_size("member")
    _, own_steps, row_count, _ = hidden.shape
    steps = heads * own_steps
    feature_count = heads * output_weight.shape[0]
    query_scale = noise_scale / math.sqrt(model)
    output_scale = noise_scale / math.sqrt(feature_count)
    bounds = [0]
    for share in SHARES:
        bounds.append(bounds[-1] + row_count // share)

    local = hidden[0].transpose(1, 0, 2)
    first_landed = first_blocks(local[: bounds[1]], heads)

    def gather_rest(landed):
        gathered = []
        for first_row, end_row in zip(bounds[1:], bounds[2:] + [None]):
            blocks = dict(landed)
            for m in range(3, heads, 2):
                blocks[m] = crossed(blocks[m - 1], "head", 1)
            gathered.append(jnp.stack([blocks[m] for m in range(heads)]))
            if end_row is not None:
                own, _ = lax.optimization_barrier((local[first_row:end_row], landed))
                landed = first_blocks(own, heads)
        return gathered

    factors = jnp.concatenate(
        [query_left, output_right, query_right * fitness[0], output_left * fitness[0]], axis=2
    ).astype(jnp.bfloat16)
    every, distance = factors[0], 1
    if members & (members - 1):
        every = lax.all_gather(every, "member", axis=0, tiled=True)
        distance = members

    right_padded = jnp.pad(
        (query_right[0] * query_scale).reshape(-1, kv_count, q_width),
        ((0, 0), (0, 0), (0, kv_width - q_width)),
    ).reshape(-1, kv_count * kv_width)
    flat_weight = joined_weight.reshape(model, kv_count * kv_width)
    out_factor = output_right[0] * output_scale
    pair_count = key_cache.shape[-1] // 128
    keys = key_cache[0].reshape(kv_count, row_count, pair_count, 128)
    values = value_cache[0].reshape(kv_count, row_count, pair_count, 128)
    flat_weight, keys, values, out_factor, first_landed = lax.optimization_barrier(
        (flat_weight, keys, values, out_factor, first_landed)
    )
    gathered = gather_rest(first_landed)
    in_weight = (flat_weight.astype(jnp.float32) + outer_sum(query_left[0], right_padded)).astype(
        jnp.bfloat16
    )
    out_weight = (
        output_weight.T.astype(jnp.float32)
        + outer_sum(out_factor, output_left[0])
    ).astype(jnp.bfloat16)

    half_dim = HEAD_DIM // 2
    exponents = jnp.arange(half_dim, dtype=jnp.float32) * (-2.0 / HEAD_DIM)
    frequency = jnp.power(jnp.float32(rotary_base), exponents)
    owners = lax.axis_index("head") ^ jnp.arange(heads, dtype=jnp.int32)
    step_ids = (owners[:, None] * own_steps + jnp.arange(own_steps, dtype=jnp.int32)).reshape(-1)
    positions = lengths[0][:, None] + step_ids[None, :]
    angles = positions.astype(jnp.float32)[..., None] * frequency
    cosines = jnp.cos(angles)
    sines = jnp.sin(angles)
    cosines = jnp.concatenate([cosines, cosines, cosines, cosines], axis=-1)
    sines = jnp.concatenate([-sines, sines, -sines, sines], axis=-1)
    late = jnp.where(step_ids[None, :] <= step_ids[:, None], 0.0, masked_score)
    late = jnp.broadcast_to(late[None], (group, steps, steps)).reshape(group * steps, steps)
    late = late.astype(jnp.float32)
    sinks = jnp.broadcast_to(
        (sink_logits * LOG2E).reshape(kv_count, group, 1, 1), (kv_count, group, steps, 128)
    ).reshape(kv_count, group * steps, 128)

    pieces = []
    partial, hopped = None, None
    for c, (first_row, end_row) in enumerate(zip(bounds[:-1], bounds[1:])):
        chunk = end_row - first_row
        token_rows = gathered[c].reshape(-1, model)
        if partial is not None:
            token_rows, partial = lax.optimization_barrier((token_rows, partial))
        projected = jnp.dot(token_rows, in_weight, preferred_element_type=jnp.float32)
        projected = projected.reshape(heads, chunk, own_steps, kv_count * kv_width)
        if own_steps % 8:
            projected = projected.transpose(1, 0, 2, 3).reshape(1, chunk, steps, kv_count * kv_width)
        attended = attend(
            first_row, projected, lengths[0], keys, values, cosines, sines, sinks, late, kv_count
        )
        landed = None if hopped is None else second_hop(*hopped)
        hopped = None if partial is None else first_hop(partial, heads)
        if distance < members:
            every = jnp.concatenate([every, crossed(every, "member", distance)], axis=0)
            distance *= 2
        attended, landed, hopped, every = lax.optimization_barrier((attended, landed, hopped, every))
        if landed is not None:
            pieces.append(total_of(*landed).reshape(-1, own_steps, model))
        flat = attended
        if own_steps % 8:
            flat = attended.reshape(chunk, heads, own_steps, -1).transpose(1, 0, 2, 3)
        flat = flat.reshape(heads * chunk * own_steps, -1)
        partial = lax.dot_general(
            flat, out_weight, (((1,), (1,)), ((), ())), preferred_element_type=jnp.float32
        ).astype(jnp.bfloat16)
        partial = partial.reshape(heads, chunk * own_steps, model)
    landed = second_hop(*hopped)
    pieces.append(total_of(*landed).reshape(-1, own_steps, model))
    landed = second_hop(*first_hop(partial, heads))
    pieces.append(total_of(*landed).reshape(-1, own_steps, model))
    layer_output = jnp.concatenate(pieces, axis=0).transpose(1, 0, 2)[None]

    while distance < members:
        every = jnp.concatenate([every, crossed(every, "member", distance)], axis=0)
        distance *= 2
    row_share, columns = query_master.shape
    row_start = lax.axis_index("member") * row_share
    left_query = lax.dynamic_slice_in_dim(every, row_start, row_share, 1)
    left_output = lax.dynamic_slice_in_dim(every, model + row_start, row_share, 1)
    right_query = every[:, 2 * model : 2 * model + columns]
    right_output = every[:, 2 * model + columns :]

    def stepped(left, right):
        total = lax.dot_general(
            left, right, (((0,), (0,)), ((), ())), preferred_element_type=jnp.float32
        )
        return total / members

    query_momenta = moment_decay * query_moment + stepped(left_query, right_query)
    output_momenta = moment_decay * output_moment + stepped(left_output, right_output)
    query_weights = query_master + learn_rate * query_momenta
    output_weights = output_master + learn_rate * output_momenta
    return (layer_output, query_weights, query_momenta, output_weights, output_momenta)


def layer_kernel(
    heads,
    members,
    bounds,
    kv_count,
    scales,
    length_ref,
    sink_ref,
    own_ref,
    weight_hbm,
    key_hbm,
    value_hbm,
    out_weight_hbm,
    left_ref,
    right_ref,
    out_left_ref,
    out_right_ref,
    frequency_ref,
    factor_ref,
    out_ref,
    every_ref,
    weight_ref,
    key_ref,
    value_ref,
    out_weight_ref,
    cos_ref,
    sin_ref,
    late_ref,
    gathered,
    partial,
    from_left,
    from_right,
    projected,
    attended,
    load_sem,
    gather_sem,
    right_sem,
    left_sem,
    sum_right_sem,
    sum_left_sem,
    right_sum_sem,
    left_sum_sem,
    factor_send,
    factor_recv,
):
    me = lax.axis_index("head")
    mine = lax.axis_index("member")
    last = heads - 1
    chunks = len(bounds) - 1
    row_count = bounds[-1]
    inner = own_ref.shape[0] // row_count
    width = projected.shape[2] // kv_count
    pairs = width // 128 - 1
    out_width = pairs * 128
    steps = heads * inner
    right = {"head": jnp.minimum(me + 1, last)}
    left = {"head": jnp.maximum(me - 1, 0)}
    mesh_id = pl.DeviceIdType.MESH

    loads = [
        pltpu.make_async_copy(source, target, load_sem.at[i])
        for i, (source, target) in enumerate(
            [
                (own_ref, gathered.at[me]),
                (weight_hbm, weight_ref),
                (key_hbm, key_ref),
                (value_hbm, value_ref),
                (out_weight_hbm, out_weight_ref),
            ]
        )
    ]
    barrier = pltpu.get_barrier_semaphore()

    @pl.when(me > 0)
    def _():
        pl.semaphore_signal(barrier, inc=1, device_id=left, device_id_type=mesh_id)

    @pl.when(me < last)
    def _():
        pl.semaphore_signal(barrier, inc=1, device_id=right, device_id_type=mesh_id)

    def peer(o):
        return {"member": lax.rem(mine + o, members)}

    for o in range(1, members):
        pl.semaphore_signal(barrier, inc=1, device_id=peer(o), device_id_type=mesh_id)
    neighbours = jnp.where(me > 0, 1, 0) + jnp.where(me < last, 1, 0) + (members - 1)
    pl.semaphore_wait(barrier, neighbours)

    def push(source, target, send, receive, device):
        return pltpu.make_async_remote_copy(
            src_ref=source,
            dst_ref=target,
            send_sem=send,
            recv_sem=receive,
            device_id=device,
            device_id_type=mesh_id,
        )

    def span(c):
        return pl.ds(bounds[c] * inner, (bounds[c + 1] - bounds[c]) * inner)

    def own_copy(c, send, device):
        return push(
            own_ref.at[span(c)], gathered.at[me, span(c)], send.at[me, c], gather_sem.at[me, c], device
        )

    def block_copy(k, c, send, device):
        block = gathered.at[k, span(c)]
        return push(block, block, send.at[k, c], gather_sem.at[k, c], device)

    def send_own(c):
        @pl.when(me < last)
        def _():
            own_copy(c, right_sem, right).start()

        @pl.when(me > 0)
        def _():
            own_copy(c, left_sem, left).start()

    def forward(t, c):
        k = jnp.maximum(me - t, 0)

        @pl.when((me >= t) & (me < last))
        def _():
            block_copy(k, c, right_sem, right).wait_recv()
            block_copy(k, c, right_sem, right).start()

        n = jnp.minimum(me + t, last)

        @pl.when((me + t <= last) & (me > 0))
        def _():
            block_copy(n, c, left_sem, left).wait_recv()
            block_copy(n, c, left_sem, left).start()

    def land(c):
        for t in range(1, heads):

            @pl.when((me == last) & (me >= t))
            def _():
                block_copy(jnp.maximum(me - t, 0), c, right_sem, right).wait_recv()

            @pl.when((me == 0) & (me + t <= last))
            def _():
                block_copy(jnp.minimum(me + t, last), c, left_sem, left).wait_recv()

    def right_sum(d, c):
        return push(
            partial.at[d, span(c)],
            from_left.at[d, span(c)],
            sum_right_sem.at[d, c],
            right_sum_sem.at[d, c],
            right,
        )

    def left_sum(d, c):
        return push(
            partial.at[d, span(c)],
            from_right.at[d, span(c)],
            sum_left_sem.at[d, c],
            left_sum_sem.at[d, c],
            left,
        )

    def add_in(d, c, landed):
        total = partial[d, span(c)].astype(jnp.float32) + landed[d, span(c)].astype(jnp.float32)
        partial[d, span(c)] = total.astype(partial.dtype)

    def sum_first(c):
        @pl.when(me == 0)
        def _():
            for d in range(last, 0, -1):
                right_sum(d, c).start()

        @pl.when(me == last)
        def _():
            for d in range(last):
                left_sum(d, c).start()

    def right_next(c):
        for d in range(last, 1, -1):

            @pl.when((me > 0) & (me < d))
            def _():
                right_sum(d, c).wait_recv()
                add_in(d, c, from_left)
                right_sum(d, c).start()

    def left_next(c):
        for d in range(last - 1):

            @pl.when((me < last) & (me > d))
            def _():
                left_sum(d, c).wait_recv()
                add_in(d, c, from_right)
                left_sum(d, c).start()

    def sum_near(c):
        @pl.when(2 * me < last)
        def _():
            right_next(c)

        @pl.when(2 * me >= last)
        def _():
            left_next(c)

    def sum_far(c):
        @pl.when(2 * me < last)
        def _():
            left_next(c)

        @pl.when(2 * me >= last)
        def _():
            right_next(c)

    def sum_last(c):
        total = partial[me, span(c)].astype(jnp.float32)

        @pl.when(me > 0)
        def _():
            right_sum(me, c).wait_recv()

        @pl.when(me < last)
        def _():
            left_sum(me, c).wait_recv()

        @pl.when((me > 0) & (me < last))
        def _():
            both = from_left[me, span(c)].astype(jnp.float32)
            both = both + from_right[me, span(c)].astype(jnp.float32)
            out_ref[span(c)] = (total + both).astype(out_ref.dtype)

        @pl.when(me == 0)
        def _():
            out_ref[span(c)] = (total + from_right[me, span(c)].astype(jnp.float32)).astype(out_ref.dtype)

        @pl.when(me == last)
        def _():
            out_ref[span(c)] = (total + from_left[me, span(c)].astype(jnp.float32)).astype(out_ref.dtype)

    def factor_copy(o):
        return push(factor_ref, every_ref.at[mine], factor_send.at[o], factor_recv.at[o], peer(o))

    send_own(0)
    if chunks > 1:
        send_own(1)
    for o in range(1, members):
        factor_copy(o).start()
    for load in loads:
        load.start()
    every_ref[mine] = factor_ref[...]

    lane = lax.broadcasted_iota(jnp.int32, (steps, 128), 1)
    low = lane < HEAD_DIM
    first = (lane & (HEAD_DIM - 1)) < HEAD_DIM // 2
    score_scale = HEAD_DIM ** (-0.5) * LOG2E
    transposed = (((1,), (1,)), ((), ()))
    one = jnp.ones((), jnp.bfloat16)
    group = 2 * pairs
    pair_count = key_ref.shape[2]
    slot = 2 * lax.broadcasted_iota(jnp.int32, (8, pair_count), 1)
    in_scale, out_scale = scales

    def tables(b, carry):
        step = lax.broadcasted_iota(jnp.int32, (steps, 128), 0)
        angles = (step + length_ref[b]).astype(jnp.float32) * frequency_ref[...]
        cos_ref[b] = jnp.cos(angles)
        sines = jnp.sin(angles)
        sin_ref[b] = jnp.where(first, -sines, sines)
        return carry

    lax.fori_loop(0, row_count, tables, 0)
    query_step = lax.broadcasted_iota(jnp.int32, (steps, steps), 0)
    new_step = lax.broadcasted_iota(jnp.int32, (steps, steps), 1)
    late = jnp.where(new_step <= query_step, 0.0, masked_score).astype(jnp.float32)
    for i in range(group):
        late_ref[i * steps : (i + 1) * steps] = late
    in_left = left_ref[...].astype(jnp.bfloat16)
    out_left = out_left_ref[...].astype(jnp.bfloat16)

    def project(c):
        size = (bounds[c + 1] - bounds[c]) * inner
        x = gathered[:, span(c), :].reshape(heads * size, -1)
        thin = lax.dot_general(x, in_left, transposed, preferred_element_type=jnp.float32)
        thin = thin.astype(jnp.bfloat16)
        for j in range(kv_count):
            columns = slice(j * width, (j + 1) * width)
            tile = jnp.dot(x, weight_ref[:, columns], preferred_element_type=jnp.float32)
            factor = right_ref[:, j * out_width : (j + 1) * out_width] * in_scale
            high, rest = split(factor)
            extra = jnp.dot(thin, high, preferred_element_type=jnp.float32)
            extra = extra + jnp.dot(thin, rest, preferred_element_type=jnp.float32)
            query = tile[:, :out_width] + extra
            start = j * width
            projected[:, :size, start : start + out_width] = query.reshape(heads, size, -1)
            projected[:, :size, start + out_width : start + width] = tile[:, out_width:].reshape(
                heads, size, -1
            )

    def attend_one(b, s, j):
        place = pl.ds(pl.multiple_of(s * inner, inner), inner)
        x = projected[:, place, j * width : (j + 1) * width].reshape(steps, width)
        cosines = cos_ref[b]
        sines = sin_ref[b]

        def rotated(block):
            swapped = jnp.where(first, pltpu.roll(block, 96, 1), pltpu.roll(block, 32, 1))
            return block * cosines + swapped * sines

        even_rows, odd_rows = [], []
        zero = jnp.zeros((steps, 128), jnp.float32)
        for i in range(pairs):
            turned = rotated(x[:, 128 * i : 128 * i + 128]) * score_scale
            other = pltpu.roll(turned, 64, 1)
            even_rows += [jnp.where(low, turned, zero), jnp.where(low, other, zero)]
            odd_rows += [jnp.where(low, zero, other), jnp.where(low, zero, turned)]
        query_even = jnp.concatenate(even_rows, axis=0).astype(jnp.bfloat16)
        query_odd = jnp.concatenate(odd_rows, axis=0).astype(jnp.bfloat16)
        pair = x[:, 128 * pairs :]
        fresh = jnp.where(low, rotated(pair), pair).astype(jnp.bfloat16)
        new_scores = lax.dot_general(query_even, fresh, transposed, preferred_element_type=jnp.float32)
        new_scores = new_scores + late_ref[...]
        sink = jnp.concatenate(
            [jnp.full((steps, 1), sink_ref[j * group + i] * LOG2E) for i in range(group)], axis=0
        )
        fresh_odd = jnp.where(low, one, fresh)
        keys = key_ref[j, b]
        values = value_ref[j, b]
        filled = length_ref[b]
        even_bias = jnp.where(slot < filled, 0.0, masked_score)[0:1]
        odd_bias = jnp.where(slot + 1 < filled, 0.0, masked_score)[0:1]
        low_lane = lax.broadcasted_iota(jnp.int32, values.shape, 1) < HEAD_DIM
        even = lax.dot_general(query_even, keys, transposed, preferred_element_type=jnp.float32)
        odd = lax.dot_general(query_odd, keys, transposed, preferred_element_type=jnp.float32)
        even = even + even_bias
        odd = odd + odd_bias
        top = jnp.max(jnp.maximum(even, odd), axis=1, keepdims=True)
        top = jnp.maximum(top, jnp.max(new_scores, axis=1, keepdims=True))
        top = jnp.maximum(top, sink)
        even = jnp.exp2(even - top).astype(jnp.bfloat16)
        odd = jnp.exp2(odd - top).astype(jnp.bfloat16)
        new = jnp.exp2(new_scores - top).astype(jnp.bfloat16)
        from_even = jnp.dot(even, jnp.where(low_lane, values, one), preferred_element_type=jnp.float32)
        from_odd = jnp.dot(odd, jnp.where(low_lane, one, values), preferred_element_type=jnp.float32)
        from_odd = from_odd + jnp.dot(new, fresh_odd, preferred_element_type=jnp.float32)
        mixed = from_even + pltpu.roll(from_odd, 64, 1)
        swapped = pltpu.roll(mixed, 64, 1)
        sink_part = jnp.exp2(sink - top)
        for i in range(pairs):
            near = slice(2 * i * steps, (2 * i + 1) * steps)
            far = slice((2 * i + 1) * steps, (2 * i + 2) * steps)
            upper = jnp.where(low, mixed[near], swapped[far])
            total = jnp.where(low, swapped[near] + sink_part[near], mixed[far] + sink_part[far])
            start = j * out_width + 128 * i
            attended[:, place, start : start + 128] = (upper / total).reshape(heads, inner, 128)

    def put_out(c):
        size = (bounds[c + 1] - bounds[c]) * inner
        x = attended[:, :size].reshape(heads * size, -1).astype(jnp.bfloat16)
        thin = lax.dot_general(x, out_left, transposed, preferred_element_type=jnp.float32)
        thin = thin.astype(jnp.bfloat16)
        model = out_weight_ref.shape[0]
        for start in range(0, model, 768):
            columns = slice(start, min(start + 768, model))
            tile = lax.dot_general(
                x, out_weight_ref[columns], transposed, preferred_element_type=jnp.float32
            )
            high, rest = split(out_right_ref[:, columns] * out_scale)
            tile = tile + jnp.dot(thin, high, preferred_element_type=jnp.float32)
            tile = tile + jnp.dot(thin, rest, preferred_element_type=jnp.float32)
            partial[:, span(c), columns] = tile.astype(partial.dtype).reshape(heads, size, -1)

    for c in range(chunks):
        if c == 0:
            for t in range(1, heads - 1):
                forward(t, c)
            for n in range(2, min(AHEAD, chunks)):
                send_own(n)
            loads[0].wait()
        elif c + AHEAD - 1 < chunks:
            send_own(c + AHEAD - 1)
        land(c)
        if c == 0:
            loads[1].wait()
        project(c)
        if c == 0:
            loads[2].wait()
            loads[3].wait()
        count = bounds[c + 1] - bounds[c]

        def attend_rows(s, carry):
            for j in range(kv_count):
                attend_one(bounds[c] + s, s, j)
            if c + 1 < chunks and heads > 2:

                @pl.when(s == max(count - 2, 0))
                def _():
                    forward(1, c + 1)

            return carry

        lax.fori_loop(0, count, attend_rows, 0)
        if c == 0:
            loads[4].wait()
        put_out(c)
        sum_first(c)
        if c > 0:
            sum_near(c - 1)
        if c + 1 < chunks:
            for t in range(2, heads - 1):
                forward(t, c + 1)
        if c > 1:
            sum_far(c - 2)
    if chunks > 1:
        sum_far(chunks - 2)
    sum_near(chunks - 1)
    sum_far(chunks - 1)
    for c in range(max(chunks - 2, 0)):
        sum_last(c)
    for o in range(1, members):
        factor_copy(o).wait_recv()
    for c in range(max(chunks - 2, 0), chunks):
        sum_last(c)

    for o in range(1, members):
        factor_copy(o).wait_send()
    for c in range(chunks):

        @pl.when(me < last)
        def _():
            own_copy(c, right_sem, right).wait_send()

        @pl.when(me > 0)
        def _():
            own_copy(c, left_sem, left).wait_send()

        for k in range(heads):

            @pl.when((k < me) & (me < last))
            def _():
                block_copy(k, c, right_sem, right).wait_send()

            @pl.when((k > me) & (me > 0))
            def _():
                block_copy(k, c, left_sem, left).wait_send()

            @pl.when(k > me)
            def _():
                right_sum(k, c).wait_send()

            @pl.when(k < me)
            def _():
                left_sum(k, c).wait_send()


def whole_layer(operands, heads, members, bounds, kv_count, scales):
    own, weight, keys, out_weight = operands[2], operands[3], operands[4], operands[6]
    row_count = bounds[-1]
    tokens, model = own.shape
    features = out_weight.shape[1]
    inner = tokens // row_count
    steps = heads * inner
    chunks = len(bounds) - 1
    rows = inner * max(b - a for a, b in zip(bounds, bounds[1:]))
    group = features // (kv_count * HEAD_DIM)
    factor = operands[-1]
    vmem = pl.BlockSpec(memory_space=pltpu.VMEM)
    smem = pl.BlockSpec(memory_space=pltpu.SMEM)
    anywhere = pl.BlockSpec(memory_space=pl.ANY)
    dma = pltpu.SemaphoreType.DMA
    block = pltpu.VMEM((heads, tokens, model), jnp.bfloat16)
    return pl.pallas_call(
        functools.partial(layer_kernel, heads, members, bounds, kv_count, scales),
        in_specs=[smem, smem, vmem] + [anywhere] * 4 + [vmem] * 6,
        out_specs=[vmem, vmem],
        out_shape=[
            jax.ShapeDtypeStruct((tokens, model), jnp.bfloat16),
            jax.ShapeDtypeStruct((members,) + factor.shape, jnp.bfloat16),
        ],
        scratch_shapes=[
            pltpu.VMEM(weight.shape, jnp.bfloat16),
            pltpu.VMEM(keys.shape, jnp.bfloat16),
            pltpu.VMEM(keys.shape, jnp.bfloat16),
            pltpu.VMEM(out_weight.shape, jnp.bfloat16),
            pltpu.VMEM((row_count, steps, 128), jnp.float32),
            pltpu.VMEM((row_count, steps, 128), jnp.float32),
            pltpu.VMEM((group * steps, steps), jnp.float32),
            block,
            block,
            block,
            block,
            pltpu.VMEM((heads, rows, weight.shape[1]), jnp.float32),
            pltpu.VMEM((heads, rows, features), jnp.float32),
            dma((5,)),
        ]
        + [dma((heads, chunks))] * 7
        + [dma((members,))] * 2,
        compiler_params=pltpu.CompilerParams(
            collective_id=0, has_side_effects=True, vmem_limit_bytes=VMEM_LIMIT
        ),
    )(*operands)


def fused_shards(
    hidden,
    joined_weight,
    output_weight,
    key_cache,
    value_cache,
    sink_logits,
    lengths,
    query_left,
    query_right,
    output_left,
    output_right,
    fitness,
    query_master,
    query_moment,
    output_master,
    output_moment,
):
    model, kv_count, kv_width = joined_weight.shape
    group = kv_width // HEAD_DIM - 2
    q_width = group * HEAD_DIM
    heads = lax.axis_size("head")
    members = lax.axis_size("member")
    _, own_steps, row_count, _ = hidden.shape
    steps = heads * own_steps
    feature_count = heads * output_weight.shape[0]
    query_scale = noise_scale / math.sqrt(model)
    output_scale = noise_scale / math.sqrt(feature_count)
    own = hidden[0].transpose(1, 0, 2).reshape(row_count * own_steps, model)
    factors = jnp.concatenate(
        [query_left, output_right, query_right * fitness[0], output_left * fitness[0]], axis=2
    ).astype(jnp.bfloat16)
    flat_weight = joined_weight.reshape(model, kv_count * kv_width)
    pair_count = key_cache.shape[-1] // 128
    keys = key_cache[0].reshape(kv_count, row_count, pair_count, 128)
    values = value_cache[0].reshape(kv_count, row_count, pair_count, 128)
    half_dim = HEAD_DIM // 2
    exponents = (jnp.arange(128, dtype=jnp.int32) % half_dim).astype(jnp.float32) * (-2.0 / HEAD_DIM)
    frequency = jnp.power(jnp.float32(rotary_base), exponents)[None]
    bounds = [0]
    for share in SIZES:
        bounds.append(bounds[-1] + row_count * share // sum(SIZES))
    if any((b - a) * own_steps % 16 or a == b for a, b in zip(bounds, bounds[1:])):
        bounds = [0, row_count]
    operands = [
        lengths[0], sink_logits, own, flat_weight, keys, values, output_weight.T,
        query_left[0], query_right[0], output_left[0], output_right[0], frequency, factors[0],
    ]
    layer_rows, every = whole_layer(
        operands, heads, members, bounds, kv_count, (query_scale, output_scale)
    )
    layer_output = layer_rows.reshape(row_count, own_steps, model).transpose(1, 0, 2)[None]
    every = every.reshape(-1, every.shape[-1])

    row_share, columns = query_master.shape
    row_start = lax.axis_index("member") * row_share
    left_query = lax.dynamic_slice_in_dim(every, row_start, row_share, 1)
    left_output = lax.dynamic_slice_in_dim(every, model + row_start, row_share, 1)
    right_query = every[:, 2 * model : 2 * model + columns]
    right_output = every[:, 2 * model + columns :]

    def stepped(left, right):
        total = lax.dot_general(
            left, right, (((0,), (0,)), ((), ())), preferred_element_type=jnp.float32
        )
        return total / members

    query_momenta = moment_decay * query_moment + stepped(left_query, right_query)
    output_momenta = moment_decay * output_moment + stepped(left_output, right_output)
    query_weights = query_master + learn_rate * query_momenta
    output_weights = output_master + learn_rate * output_momenta
    return (layer_output, query_weights, query_momenta, output_weights, output_momenta)


def layer(hidden, *others):
    body = fused_shards if hidden.shape[1] % 8 == 0 else shards
    return body(hidden, *others)


def solution(mesh):
    placed = (
        P("member", "head", None, None),
        P(None, "head", None),
        P("head", None),
        P("member", "head", None, None),
        P("member", "head", None, None),
        P("head"),
        P("member", None),
        P("member", None, None),
        P("member", None, "head"),
        P("member", None, "head"),
        P("member", None, None),
        P("member"),
        P("member", "head"),
        P("member", "head"),
        P("member", "head"),
        P("member", "head"),
    )
    return jax.shard_map(
        layer,
        mesh=mesh,
        in_specs=placed,
        out_specs=(
            P("member", "head", None, None),
            P("member", "head"),
            P("member", "head"),
            P("member", "head"),
            P("member", "head"),
        ),
        check_vma=False,
    )
```
